512 devices in a mesh: seq: 32 (over z, core), head: 16 (over x, y).
Axes of the slice: x: 4, y: 4, z: 16, core: 2. Of those that a mesh axis runs over, the one named last changes fastest.
Arguments:
- tokens: bfloat16 [2048, 3072], P(('seq', 'head')), may hold values from -6 to 6
- w_qkv: bfloat16 [3, 3072, 3072], P(None, 'head'), may hold values from -0.109375 to 0.109375
- lr_weight: bfloat16 [48, 3072], P('head'), may hold values from -0.21875 to 0.21875
- lr_base: float32 [48], P('head'), may hold values from 0.3 to 3
- conv_weight: float32 [2, 4, 3072], P(None, None, 'head'), may hold values from -3 to 3
- w_init: float32 [2, 48, 64, 64], P(None, 'head'), may hold values from -0.75 to 0.75
- w_out: bfloat16 [3072, 3072], P('head'), may hold values from -0.15625 to 0.15625
Outputs:
- mixed: bfloat16 [2048, 3072], P(('seq', 'head'))
The draws below stay inside these ranges and needn't reach their ends.
All inputs are finite; a program needn't handle non-finite values.
Results may differ from the reference program's by a relative error of at most 0.018.
Values may be sent and summed in bfloat16 or wider, within the bound.
No kernel may reach another device: no remote copies, remote signals or barrier semaphores. Data moves between devices by JAX's collectives and lax.ppermute only.
A program may use at most 128 MiB of HBM per device.

```python
import math
import jax
import jax.numpy as jnp
from jax import lax

D = 3072
HEADS = 48
HD = 64
MB = 16
KERNEL = 4
TOKENS = 2048
INNER = 3072
HEAD_DEV = 3
NMB = 128
N_HEAD = 16


def raised(values, own_key, source, target, blocks, factor):
    owner, partner = [(jnp.arange(values.shape[dim]) // (values.shape[dim] // blocks)).reshape([-1 if axis == dim else 1 for axis in range(values.ndim)]) for dim in (source, target)]
    chosen = jax.random.permutation(own_key, blocks)[partner]
    strong = (owner == chosen) | (owner == (partner + blocks // 2) % blocks)
    return jnp.where(strong, factor * values, values)


def block_scale(own_key, dims, split, smallest, largest):
    loudness, own = 1.0, jax.random.fold_in(own_key, 6)
    for dim, shards_of in split:
        steps = jnp.exp(jax.random.uniform(jax.random.fold_in(own, dim), (shards_of,), jnp.float32, smallest / len(split), largest / len(split)))
        loudness = loudness * jnp.repeat(steps, dims[dim] // shards_of).reshape([-1 if axis == dim else 1 for axis in range(len(dims))])
    return loudness


def gaussian(stream_key, extent, width, limit, split=(), kind=jnp.bfloat16):
    values = width * jax.random.normal(stream_key, extent, jnp.float32)
    if split:
        values = values * block_scale(stream_key, extent, split, -0.22, 0.18)
    return jnp.clip(values, -limit, limit).astype(kind)


def bell_draw_with(own_key, shape, width, limit, split, heavy, kind=jnp.bfloat16):
    entries = width * jax.random.normal(own_key, shape, jnp.float32)
    if split:
        entries = entries * block_scale(own_key, shape, split, -0.22, 0.18)
    return jnp.clip(raised(entries, jax.random.fold_in(own_key, 3), *heavy), -limit, limit).astype(kind)


def setup_inputs(seed: int = 0) -> dict:
    streams_of = jax.random.split(jax.random.key(seed), 8)
    tokens = gaussian(streams_of[0], (TOKENS, D), 1.0, 6.0, ((0, 512),))
    w_qkv = gaussian(streams_of[1], (3, INNER, D), D ** -0.5, 0.109375, ((1, 16),))
    lr_weight = gaussian(streams_of[2], (HEADS, D), (D // 4) ** -0.5, 0.21875, ((0, 16),))
    lr_base = jnp.clip(jnp.exp(math.log(3.0) - 2.3025851 * jax.random.uniform(streams_of[3], (HEADS,), jnp.float32) ** block_scale(streams_of[3], (HEADS,), ((0, 16),), -0.2, 0.2)), 0.3, 3.0)
    conv_weight = gaussian(streams_of[4], (2, KERNEL, INNER), 0.5, 3.0, ((2, 16),), jnp.float32)
    w_init = gaussian(streams_of[5], (2, HEADS, HD, HD), HD ** -0.5, 0.75, ((1, 16),), jnp.float32)
    w_out = bell_draw_with(streams_of[6], (INNER, D), INNER ** -0.5, 0.15625, ((0, 16),), (0, 1, 16, 2.0))
    return {"tokens": tokens, "w_qkv": w_qkv, "lr_weight": lr_weight, "lr_base": lr_base, "conv_weight": conv_weight, "w_init": w_init, "w_out": w_out}


PRECISE = lax.Precision.HIGHEST
EPSILON = 1e-05

def compose_maps(earlier_map, later_map):
    return (jnp.matmul(earlier_map[0], later_map[0], precision=PRECISE), jnp.matmul(earlier_map[1], later_map[0], precision=PRECISE) + later_map[1])

def batch_terms(keys_unit, value_rows, step_rates):
    scaled = step_rates[..., None] * keys_unit
    identity_mat = jnp.eye(keys_unit.shape[-1], dtype=jnp.float32)
    transition = identity_mat - jnp.einsum('...thc,...thd->...hcd', scaled, keys_unit, precision=PRECISE)
    offset = jnp.einsum('...thv,...thc->...hvc', value_rows, scaled, precision=PRECISE)
    return (transition, offset)

def batch_output(inner_state, queries, keys_unit, value_rows, step_rates, token_mask):
    applied_q = jnp.einsum('...hvc,...thc->...thv', inner_state, queries, precision=PRECISE)
    applied_k = jnp.einsum('...hvc,...thc->...thv', inner_state, keys_unit, precision=PRECISE)
    errors = applied_k - value_rows
    scores = jnp.einsum('...thc,...shc->...hts', queries, keys_unit, precision=PRECISE)
    scores = scores * token_mask * jnp.swapaxes(step_rates, -1, -2)[..., :, None, :]
    return applied_q - jnp.einsum('...hts,...shv->...thv', scores, errors, precision=PRECISE)

def layer_norm(inputs):
    average = lax.optimization_barrier(jnp.mean(inputs, axis=-1, keepdims=True))
    centred = inputs - average
    variance = lax.optimization_barrier(jnp.mean(centred * centred, axis=-1, keepdims=True))
    return centred / jnp.sqrt(variance + EPSILON)

def causal_conv(raw_rows, taps_row):
    padded = jnp.concatenate([jnp.zeros((KERNEL - 1, raw_rows.shape[1]), jnp.float32), raw_rows.astype(jnp.float32)], axis=0)
    running = jnp.zeros(raw_rows.shape, jnp.float32)
    for position in range(KERNEL):
        running = running + taps_row[position][None, :] * padded[position:position + TOKENS]
    return running

def reference(tokens, w_qkv, lr_weight, lr_base, conv_weight, w_init, w_out):
    projected = [jnp.dot(tokens, jnp.transpose(w_qkv[number]), preferred_element_type=jnp.float32).astype(jnp.bfloat16) for number in range(3)]
    lr_logit = jnp.dot(tokens, jnp.transpose(lr_weight), preferred_element_type=jnp.float32)
    queries = causal_conv(projected[0], conv_weight[0]).reshape(NMB, MB, HEADS, HD)
    keys_conv = causal_conv(projected[1], conv_weight[1]).reshape(TOKENS, HEADS, HD)
    keys_unit = keys_conv / jnp.sqrt((lax.optimization_barrier(jnp.mean(keys_conv * keys_conv, axis=-1, keepdims=True)) + EPSILON) * HD)
    keys_unit = keys_unit.reshape(NMB, MB, HEADS, HD)
    value_rows = projected[2].astype(jnp.float32).reshape(NMB, MB, HEADS, HD)
    step_rates = (lr_base[None, :] * jax.nn.sigmoid(lr_logit) / MB).reshape(NMB, MB, HEADS)
    causal_mask = (jnp.arange(MB)[:, None] >= jnp.arange(MB)[None, :]).astype(jnp.float32)
    anti_mask = jnp.transpose(causal_mask)

    def make_step(token_mask):

        def step_fn(inner_state, minibatch):
            queries_b, keys_b, values_b, rates_b = minibatch
            result = batch_output(inner_state, queries_b, keys_b, values_b, rates_b, token_mask)
            transition, offset = batch_terms(keys_b, values_b, rates_b)
            return (jnp.matmul(inner_state, transition, precision=PRECISE) + offset, result)
        return step_fn
    inputs_all = (queries, keys_unit, value_rows, step_rates)
    unused_f, fwd_out = lax.scan(make_step(causal_mask), w_init[0], inputs_all)
    unused_r, rev_out = lax.scan(make_step(anti_mask), w_init[1], inputs_all, reverse=True)
    hidden = (layer_norm(fwd_out) + layer_norm(rev_out)).reshape(TOKENS, INNER).astype(jnp.bfloat16)
    grouped = jnp.transpose(hidden.reshape(TOKENS, N_HEAD, HEAD_DEV * HD), (1, 0, 2))
    weights = w_out.reshape(N_HEAD, HEAD_DEV * HD, D)

    def add_group(running, group_pair):
        rounded = jnp.dot(group_pair[0], group_pair[1], preferred_element_type=jnp.float32).astype(jnp.bfloat16)
        rounded = lax.optimization_barrier(rounded)
        return (running + rounded.astype(jnp.float32), None)
    summed, unused_g = lax.scan(add_group, jnp.zeros((TOKENS, D), jnp.float32), (grouped, weights))
    return summed.astype(jnp.bfloat16)
```

```python
import jax
import jax.numpy as jnp
from jax import lax
from jax.experimental import pallas as pl
from jax.experimental.pallas import tpu as pltpu
from jax.sharding import PartitionSpec as P

MB = 16
KERNEL = 4
EPSILON = 1e-05
F32 = jnp.float32
BF16 = jnp.bfloat16


def mm(a, b, ca=1, cb=0):
    return lax.dot_general(a, b, (((ca,), (cb,)), ((), ())), preferred_element_type=F32)


def local_kernel(own_ref, mate_ref, halo0_ref, halo1_ref, w_ref, lrw_ref, base_ref, taps_ref,
                 maps_ref, qeff_ref, oeff_ref, xall_ref, wide_ref, lrp_ref):
    core = lax.axis_index("seq") % 2
    half = w_ref.shape[2] // 2
    tokens = own_ref.shape[0] // 2

    def spread(src, row, count):
        for j in range(half // 128):
            wide_ref[j, 0:2 * count, :] = src[:, j * 128:(j + 1) * 128].astype(F32)
            for part in range(2):
                xall_ref[pl.ds(row, count), part * half + j * 128:part * half + (j + 1) * 128] = (
                    wide_ref[j, pl.ds(part, count, stride=2), :].astype(BF16))

    spread(own_ref[...], pl.multiple_of(core * tokens, 64), tokens)
    spread(mate_ref[...], pl.multiple_of((1 - core) * tokens, 64), tokens)
    halo = jnp.where(core == 0, halo0_ref[...].astype(F32), halo1_ref[...].astype(F32))
    for j in range(half // 128):
        wide_ref[j, 0:8, :] = halo[:, j * 128:(j + 1) * 128]
        for part in range(2):
            xall_ref[128:144, part * half + j * 128:part * half + (j + 1) * 128] = (
                wide_ref[j, pl.ds(part, 16, stride=2), :].astype(BF16))
    lrp_ref[...] = jnp.zeros_like(lrp_ref)
    lrp_ref[0:3, :] = lrw_ref[...]

    inner = w_ref.shape[1]
    rows = jnp.concatenate([w_ref[...].reshape(3 * inner, 2 * half), lrp_ref[...]], axis=0)
    proj = mm(rows, xall_ref[0:256, :], 1, 1)

    lane = lax.broadcasted_iota(jnp.int32, (2 * inner, 128), 1)
    qk = proj[0:2 * inner, 0:128].astype(BF16).astype(F32)
    edge = proj[0:2 * inner, 128:256].astype(BF16).astype(F32)
    taps = taps_ref[...]
    conv = taps[:, KERNEL - 1:KERNEL] * qk
    for back in range(1, KERNEL):
        moved = jnp.where(lane < back, pltpu.roll(edge, (back - 4) % 128, 1), pltpu.roll(qk, back, 1))
        conv = conv + taps[:, KERNEL - 1 - back:KERNEL - back] * moved
    values = proj[2 * inner:3 * inner, 0:128].astype(BF16)
    gate = jax.nn.sigmoid(proj[3 * inner:3 * inner + 8, 0:128])

    sign = 1 - 2 * core
    src = lax.broadcasted_iota(jnp.int32, (128, 128), 0)
    dst = lax.broadcasted_iota(jnp.int32, (128, 128), 1)
    seen = sign * (dst - src) >= 0
    strict = sign * (dst // MB - src // MB) > 0
    eye = jnp.where(src == dst, 1.0, 0.0).astype(F32)

    heads = inner // 64
    for h in range(heads):
        lo, hi = h * 64, (h + 1) * 64
        q = conv[lo:hi]
        k = conv[inner + lo:inner + hi]
        k = k * lax.rsqrt((jnp.mean(k * k, axis=0, keepdims=True) + EPSILON) * 64)
        rate = gate[h:h + 1] * (base_ref[h] / MB)
        kb = k.astype(BF16)
        krb = (k * rate).astype(BF16)
        krt = krb.T
        v = values[lo:hi]
        grams = mm(krt, jnp.concatenate([kb, q.astype(BF16)], axis=1))
        u = jnp.where(strict, grams[:, 0:128], 0.0)
        s = jnp.where(seen, grams[:, 128:256], 0.0)
        ub = u.astype(BF16)
        u2 = mm(ub, ub)
        u2b = u2.astype(BF16)
        u4 = mm(u2b, u2b)
        t1 = eye - u + u2 - mm(ub, u2b)
        t = t1 + mm(t1.astype(BF16), u4.astype(BF16))
        solved = mm(t.astype(BF16), jnp.concatenate([s.astype(BF16), krt], axis=1)).astype(BF16)
        both = mm(jnp.concatenate([kb, v], axis=0), solved)
        maps_ref[lo:hi, :] = jnp.concatenate([-both[0:64, 128:192], both[64:128, 128:192]], axis=1).astype(BF16)
        qeff_ref[lo:hi, :] = (q - both[0:64, 0:128]).astype(BF16)
        oeff_ref[lo:hi, :] = both[64:128, 0:128]


def chain_kernel(maps_ref, qeff_ref, oeff_ref, init_ref, out_ref):
    place = lax.axis_index("seq")
    core = place % 2
    chip = place // 2
    chips = maps_ref.shape[0]
    steps = jnp.where(core == 0, chip, chips - 1 - chip)
    heads = init_ref.shape[1]
    states = [init_ref[core, h] for h in range(heads)]
    for i in range(chips - 1):
        at = jnp.where(core == 0, i, chips - 1 - i)
        live = i < steps
        for h in range(heads):
            block = maps_ref[at, h * 64:(h + 1) * 64, :]
            new = states[h] + mm(states[h].astype(BF16), block[:, 0:64]) + block[:, 64:128].astype(F32)
            states[h] = jnp.where(live, new, states[h])
    for h in range(heads):
        lo, hi = h * 64, (h + 1) * 64
        out = mm(states[h].astype(BF16), qeff_ref[lo:hi, :]) + oeff_ref[lo:hi, :]
        centred = out - jnp.mean(out, axis=0, keepdims=True)
        variance = jnp.mean(centred * centred, axis=0, keepdims=True)
        out_ref[lo:hi, :] = centred * lax.rsqrt(variance + EPSILON)


def project_kernel(own_ref, mate_ref, w_ref, out_ref):
    core = lax.axis_index("seq") % 2
    hidden = (own_ref[...] + mate_ref[...]).astype(BF16)
    row = lax.broadcasted_iota(jnp.int32, (128, 128), 0)
    col = lax.broadcasted_iota(jnp.int32, (128, 128), 1)
    pick = jnp.where(col == row // 2 + 64 * core, 1.0, 0.0).astype(BF16)
    twice = mm(pick, hidden, 1, 1).astype(BF16)
    half = out_ref.shape[1]
    even = lax.broadcasted_iota(jnp.int32, (128, half), 0) % 2 == 0
    first = mm(twice, w_ref[:, 0:half])
    second = mm(twice, w_ref[:, half:2 * half])
    out_ref[...] = jnp.where(even, first, second).astype(BF16)


def total_kernel(parts_ref, out_ref, wide_ref):
    acc = parts_ref[0].astype(F32)
    for i in range(1, parts_ref.shape[0]):
        acc = acc + parts_ref[i].astype(F32)
    half = acc.shape[1]
    for j in range(half // 128):
        wide_ref[j] = acc[:, j * 128:(j + 1) * 128]
        for part in range(2):
            out_ref[:, part * half + j * 128:part * half + (j + 1) * 128] = (
                wide_ref[j, pl.ds(part, 4, stride=2), :].astype(BF16))


def shards(tokens, w_qkv, lr_weight, lr_base, conv_weight, w_init, w_out):
    width = tokens.shape[1]
    half = width // 2
    inner = w_qkv.shape[1]
    n_seq = lax.axis_size("seq")
    n_head = lax.axis_size("head")
    params = pltpu.CompilerParams(vmem_limit_bytes=48 * 1024 * 1024)
    vmem = pl.BlockSpec(memory_space=pltpu.VMEM)
    smem = pl.BlockSpec(memory_space=pltpu.SMEM)

    folded = jnp.broadcast_to(tokens.reshape(1, 8, half), (n_head, 8, half))
    own = lax.all_to_all(folded, "head", 0, 0)
    swap = [(i, i ^ 1) for i in range(n_seq)]
    mate = lax.ppermute(own, "seq", swap)
    tail = own[n_head - 1]
    halo0 = lax.ppermute(tail, "seq", [(i, i + 1) for i in range(1, n_seq - 1, 2)])
    halo1 = lax.ppermute(tail, "seq", [(i, i + 2) for i in range(1, n_seq - 2, 2)])
    taps = jnp.transpose(conv_weight, (0, 2, 1)).reshape(2 * inner, KERNEL)

    maps, qeff, oeff = pl.pallas_call(
        local_kernel,
        out_shape=(
            jax.ShapeDtypeStruct((inner, 128), BF16),
            jax.ShapeDtypeStruct((inner, 128), BF16),
            jax.ShapeDtypeStruct((inner, 128), F32),
        ),
        in_specs=[vmem, vmem, vmem, vmem, vmem, vmem, smem, vmem],
        out_specs=(vmem, vmem, vmem),
        scratch_shapes=[
            pltpu.VMEM((256, width), BF16),
            pltpu.VMEM((half // 128, 128, 128), F32),
            pltpu.VMEM((16, width), BF16),
        ],
        compiler_params=params,
        name="local",
    )(own.reshape(n_head * 8, half), mate.reshape(n_head * 8, half), halo0, halo1, w_qkv, lr_weight, lr_base, taps)

    groups = [list(range(c, n_seq, 2)) for c in range(2)]
    gathered = lax.all_gather(maps, "seq", axis_index_groups=groups)
    normed = pl.pallas_call(
        chain_kernel,
        out_shape=jax.ShapeDtypeStruct((inner, 128), F32),
        in_specs=[vmem] * 4,
        out_specs=vmem,
        compiler_params=params,
        name="chain",
    )(gathered, qeff, oeff, w_init)
    other = lax.ppermute(normed, "seq", swap)
    partial = pl.pallas_call(
        project_kernel,
        out_shape=jax.ShapeDtypeStruct((n_head * 8, half), BF16),
        in_specs=[vmem] * 3,
        out_specs=vmem,
        compiler_params=params,
        name="project",
    )(normed, other, w_out)
    parts = lax.all_to_all(partial.reshape(n_head, 8, half), "head", 0, 0)
    return pl.pallas_call(
        total_kernel,
        out_shape=jax.ShapeDtypeStruct(tokens.shape, BF16),
        in_specs=[vmem],
        out_specs=vmem,
        scratch_shapes=[pltpu.VMEM((half // 128, 8, 128), F32)],
        compiler_params=params,
        name="total",
    )(parts)


def solution(mesh):
    placed = (
        P(("seq", "head"), None),
        P(None, "head", None),
        P("head", None),
        P("head"),
        P(None, None, "head"),
        P(None, "head", None, None),
        P("head", None),
    )
    return jax.shard_map(
        shards, mesh=mesh, in_specs=placed, out_specs=P(("seq", "head"), None), check_vma=False
    )
```

```python
import jax
import jax.numpy as jnp
from jax import lax
from jax.experimental import pallas as pl
from jax.experimental.pallas import tpu as pltpu
from jax.sharding import PartitionSpec as P

MB = 16
KERNEL = 4
EPSILON = 1e-05
F32 = jnp.float32
BF16 = jnp.bfloat16


def mm(a, b, ca=1, cb=0):
    return lax.dot_general(a, b, (((ca,), (cb,)), ((), ())), preferred_element_type=F32)


def cat(parts, axis):
    return jnp.concatenate(parts, axis=axis)


def normed(u):
    centred = u - jnp.mean(u, axis=0, keepdims=True)
    return centred * lax.rsqrt(jnp.mean(centred * centred, axis=0, keepdims=True) + EPSILON)


def role_of(place):
    return (place + place // 2) % 2


def fold_kernel(tokens_ref, lrw_ref, conv_ref, base_ref, out_ref, lrp_ref, taps_ref, rate_ref, wide_ref):
    role = role_of(lax.axis_index("seq"))
    half = out_ref.shape[2]
    for j in range(half // 128):
        cols = slice(j * 128, (j + 1) * 128)
        for part in range(2):
            piece = tokens_ref[:, part * half + j * 128:part * half + (j + 1) * 128].astype(F32)
            wide_ref[j, pl.ds(part, 4, stride=2), :] = piece
        block = wide_ref[j].astype(BF16)
        for i in range(out_ref.shape[0]):
            out_ref[i, :, cols] = block
    lrw = lrw_ref[...].astype(F32)
    whole = jnp.where(role == 0, lrw[0:1], lrw[2:3])
    lrp_ref[...] = cat([whole, lrw[1:2], jnp.zeros((14, lrw.shape[1]), F32)], 0).astype(BF16)
    inner = conv_ref.shape[2]
    taps_rows = cat([conv_ref[0], conv_ref[1]], 0)
    taps_ref[...] = cat([taps_rows, jnp.zeros((2 * KERNEL, 256 - inner), F32)], 1).T
    base = base_ref[...] / MB
    rate_ref[0:1, :] = jnp.broadcast_to(jnp.where(role == 0, base[0:1, 0:1], base[0:1, 2:3]), (1, 128))
    rate_ref[1:2, :] = jnp.broadcast_to(base[0:1, 1:2], (1, 128))


def spread(src_ref, wide_ref, out_ref, row):
    half = src_ref.shape[1]
    for j in range(half // 128):
        wide_ref[j] = src_ref[:, j * 128:(j + 1) * 128].astype(F32)
        for part in range(2):
            cols = slice(part * half + j * 128, part * half + (j + 1) * 128)
            out_ref[pl.ds(row, 64), cols] = wide_ref[j, pl.ds(part, 64, stride=2), :].astype(BF16)


def local_kernel(own_hbm, mate_hbm, halo0_hbm, halo1_hbm, w_hbm, lrp_ref, taps_ref, rate_ref, send_ref, qeff_ref, oeff_ref,
                 own_ref, mate_ref, halo0_ref, halo1_ref, w_ref, wide_ref, tail_ref, xall_ref, sems):
    place = lax.axis_index("seq")
    core = place % 2
    role = role_of(place)
    half = halo0_ref.shape[1]
    fetches = [
        pltpu.make_async_copy(a, b, sems.at[i])
        for i, (a, b) in enumerate(((own_hbm, own_ref), (mate_hbm, mate_ref), (halo0_hbm, halo0_ref), (halo1_hbm, halo1_ref)))
    ]
    used = pl.ds(pl.multiple_of(64 * role, 64), 128)
    pieces = []
    for part in range(2):
        cols = slice(part * half, (part + 1) * half)
        pieces.append(pltpu.make_async_copy(w_hbm.at[:, used, cols], w_ref.at[:, :, cols], sems.at[4 + part]))
    for fetch in fetches + pieces:
        fetch.start()
    fetches[0].wait()
    spread(own_ref, wide_ref, xall_ref, pl.multiple_of(64 * core, 64))
    fetches[1].wait()
    spread(mate_ref, wide_ref, xall_ref, pl.multiple_of(64 * (1 - core), 64))
    fetches[2].wait()
    fetches[3].wait()
    halo = jnp.where(core == 0, halo0_ref[...].astype(F32), halo1_ref[...].astype(F32))
    for j in range(half // 128):
        tail_ref[j, 0:24, :] = jnp.zeros((24, 128), F32)
        tail_ref[j, 24:32, :] = halo[:, j * 128:(j + 1) * 128]
        for part in range(2):
            cols = slice(part * half + j * 128, part * half + (j + 1) * 128)
            xall_ref[240:256, cols] = tail_ref[j, pl.ds(part, 16, stride=2), :].astype(BF16)
    at = pl.multiple_of(128 * role, 64)
    whole = pl.ds(pl.multiple_of(64 * role, 64), 64)
    shared = pl.ds(pl.multiple_of(64 * (1 - role), 64), 64)
    mid = pl.ds(pl.multiple_of(64 - 32 * role, 32), 32)
    proj = None
    for part in range(2):
        cols = slice(part * half, (part + 1) * half)
        pieces[part].wait()
        rows = cat([
            w_ref[0, whole, cols], w_ref[0, shared, cols], w_ref[1, whole, cols], w_ref[1, shared, cols],
            w_ref[2, whole, cols], w_ref[2, mid, cols], lrp_ref[:, cols],
        ], 0)
        term = mm(rows, xall_ref[:, cols], 1, 1)
        proj = term if proj is None else proj + term
    lane = lax.broadcasted_iota(jnp.int32, (128, 128), 1)
    taps = cat([taps_ref[pl.ds(at, 64), :], taps_ref[64:128, :]], 0)
    convs = []
    for i in range(2):
        raw = proj[128 * i:128 * i + 128, 0:128].astype(BF16).astype(F32)
        edge = proj[128 * i:128 * i + 128, 128:256].astype(BF16).astype(F32)
        first = KERNEL * i
        conv = taps[:, first + KERNEL - 1:first + KERNEL] * raw
        for back in range(1, KERNEL):
            moved = jnp.where(lane < back, pltpu.roll(edge, back, 1), pltpu.roll(raw, back, 1))
            conv = conv + taps[:, first + KERNEL - 1 - back:first + KERNEL - back] * moved
        convs.append(conv)

    src = lax.broadcasted_iota(jnp.int32, (128, 128), 0)
    dst = lax.broadcasted_iota(jnp.int32, (128, 128), 1)
    strict = dst // MB > src // MB
    eye = jnp.where(src == dst, 1.0, 0.0).astype(F32)

    maps = []
    for slot in range(2):
        lo, hi = slot * 64, (slot + 1) * 64
        q = convs[0][lo:hi]
        k = convs[1][lo:hi]
        k = k * lax.rsqrt((jnp.mean(k * k, axis=0, keepdims=True) + EPSILON) * 64)
        rate = jax.nn.sigmoid(proj[352 + slot:353 + slot, 0:128]) * rate_ref[slot:slot + 1, :]
        v = proj[256:320, 0:128] if slot == 0 else proj[320:352, 0:128]
        kb = k.astype(BF16)
        kt = kb.T
        grams = mm(kt, cat([kb, q.astype(BF16)], 1))
        u = jnp.where(strict, grams[:, 0:128], 0.0) * rate
        ub = u.astype(BF16)
        u2 = mm(ub, ub)
        u2b = u2.astype(BF16)
        u4 = mm(u2b, u2b)
        t1 = eye - u + u2 - mm(ub, u2b)
        t = t1 + mm(t1.astype(BF16), u4.astype(BF16))
        rev = t.T * rate
        fwd = rev.T
        scores = grams[:, 128:256]
        seen_f = jnp.where(dst >= src, scores, 0.0).astype(BF16)
        seen_r = jnp.where(dst <= src, scores, 0.0).astype(BF16)
        solved_f = mm(fwd.astype(BF16), cat([seen_f, kt], 1)).astype(BF16)
        solved_r = mm(rev.astype(BF16), cat([seen_r, kt], 1)).astype(BF16)
        stacked = cat([kb, v.astype(BF16)], 0)
        pair = []
        for way, solved in enumerate((solved_f, solved_r)):
            both = mm(stacked, solved)
            qeff_ref[way, lo:hi, :] = (q - both[0:64, 0:128]).astype(BF16)
            oeff_ref[way, lo:lo + v.shape[0], :] = both[64:, 0:128]
            pair.append((-both[0:64, 128:192], both[64:, 128:192]))
        maps.append(pair)
    (a0, b0), (a1, b1) = maps[0][0], maps[1][0]
    send_ref[0:64, :] = cat([a0, a1], 1).astype(BF16)
    for way in range(2):
        b0, b1 = maps[0][way][1], maps[1][way][1]
        packed = cat([b0[0:48], cat([b0[48:64], b1], 0)], 1)
        send_ref[64 + 48 * way:112 + 48 * way, :] = packed.astype(BF16)


def chain_kernel(maps_ref, qeff_ref, oeff_ref, init_ref, out_ref):
    place = lax.axis_index("seq")
    role = role_of(place)
    chip = place // 2
    chips = maps_ref.shape[0]
    states = []
    for way in range(2):
        shared = init_ref[way, 1, pl.ds(pl.multiple_of(32 * role, 32), 32), :]
        states.append([init_ref[way, 2 * role], shared])
    for i in range(chips - 1):
        for way in range(2):
            j = i if way == 0 else chips - 1 - i
            live = (j < chip) if way == 0 else (j > chip)
            block = maps_ref[j]
            whole, shared = states[way]
            at = 64 + 48 * way
            b0 = cat([block[at:at + 48, 0:64], block[at:at + 16, 64:128]], 0).astype(F32)
            b1 = block[at + 16:at + 48, 64:128].astype(F32)
            new0 = whole + mm(whole.astype(BF16), block[0:64, 0:64], 1, way) + b0
            new1 = shared + mm(shared.astype(BF16), block[0:64, 64:128], 1, way) + b1
            states[way] = [jnp.where(live, new0, whole), jnp.where(live, new1, shared)]
    sums = None
    for way in range(2):
        whole = mm(states[way][0].astype(BF16), qeff_ref[way, 0:64, :]) + oeff_ref[way, 0:64, :]
        sums = normed(whole) if sums is None else sums + normed(whole)
        shared = mm(states[way][1].astype(BF16), qeff_ref[way, 64:128, :]) + oeff_ref[way, 64:96, :]
        out_ref[64 + 32 * way:96 + 32 * way, :] = shared
    out_ref[0:64, :] = sums


def output_kernel(mine_ref, mate_ref, w_ref, out_ref):
    place = lax.axis_index("seq")
    core = place % 2
    role = role_of(place)
    mine = mine_ref[...]
    mate = mate_ref[...]
    low = jnp.where(role == 0, mine, mate)
    high = jnp.where(role == 0, mate, mine)
    middle = normed(cat([low[64:96], high[64:96]], 0)) + normed(cat([low[96:128], high[96:128]], 0))
    hidden = cat([low[0:64], middle, high[0:64]], 0).astype(BF16)
    row = lax.broadcasted_iota(jnp.int32, (128, 128), 0)
    col = lax.broadcasted_iota(jnp.int32, (128, 128), 1)
    pick = jnp.where(col == row // 2 + 64 * core, 1.0, 0.0).astype(BF16)
    twice = mm(pick, hidden, 1, 1).astype(BF16)
    half = out_ref.shape[1]
    even = lax.broadcasted_iota(jnp.int32, (128, half), 0) % 2 == 0
    first = mm(twice, w_ref[:, 0:half])
    second = mm(twice, w_ref[:, half:2 * half])
    out_ref[...] = jnp.where(even, first, second).astype(BF16)


def total_kernel(parts_ref, out_ref, wide_ref):
    acc = parts_ref[0].astype(F32)
    for i in range(1, parts_ref.shape[0]):
        acc = acc + parts_ref[i].astype(F32)
    half = acc.shape[1]
    for j in range(half // 128):
        wide_ref[j] = acc[:, j * 128:(j + 1) * 128]
        for part in range(2):
            out_ref[:, part * half + j * 128:part * half + (j + 1) * 128] = (
                wide_ref[j, pl.ds(part, 4, stride=2), :].astype(BF16))


def shards(tokens, w_qkv, lr_weight, lr_base, conv_weight, w_init, w_out):
    width = tokens.shape[1]
    half = width // 2
    inner = w_qkv.shape[1]
    n_seq = lax.axis_size("seq")
    n_head = lax.axis_size("head")
    params = pltpu.CompilerParams(vmem_limit_bytes=24 * 1024 * 1024)
    vmem = pl.BlockSpec(memory_space=pltpu.VMEM)
    hbm = pl.BlockSpec(memory_space=pl.ANY)

    folded, lr_rows, taps, base = pl.pallas_call(
        fold_kernel,
        out_shape=(
            jax.ShapeDtypeStruct((n_head, 8, half), BF16),
            jax.ShapeDtypeStruct((16, width), BF16),
            jax.ShapeDtypeStruct((256, 2 * KERNEL), F32),
            jax.ShapeDtypeStruct((8, 128), F32),
        ),
        in_specs=[vmem] * 4,
        out_specs=(vmem,) * 4,
        scratch_shapes=[pltpu.VMEM((half // 128, 8, 128), F32)],
        compiler_params=params,
        name="fold",
    )(tokens, lr_weight, conv_weight, lr_base.reshape(1, lr_base.shape[0]))
    own = lax.all_to_all(folded, "head", 0, 0)
    swap = [(i, i ^ 1) for i in range(n_seq)]
    mate = lax.ppermute(own, "seq", swap)
    tail = own[n_head - 1]
    halo0 = lax.ppermute(tail, "seq", [(i, i + 1) for i in range(1, n_seq - 1, 2)])
    halo1 = lax.ppermute(tail, "seq", [(i, i + 2) for i in range(1, n_seq - 2, 2)])
    send, qeff, oeff = pl.pallas_call(
        local_kernel,
        out_shape=(
            jax.ShapeDtypeStruct((160, 128), BF16),
            jax.ShapeDtypeStruct((2, 128, 128), BF16),
            jax.ShapeDtypeStruct((2, 96, 128), F32),
        ),
        in_specs=[hbm] * 5 + [vmem] * 3,
        out_specs=(vmem, vmem, vmem),
        scratch_shapes=[
            pltpu.VMEM((n_head * 8, half), BF16),
            pltpu.VMEM((n_head * 8, half), BF16),
            pltpu.VMEM((8, half), BF16),
            pltpu.VMEM((8, half), BF16),
            pltpu.VMEM((3, 128, width), BF16),
            pltpu.VMEM((half // 128, 128, 128), F32),
            pltpu.VMEM((half // 128, 32, 128), F32),
            pltpu.VMEM((256, width), BF16),
            pltpu.SemaphoreType.DMA((6,)),
        ],
        compiler_params=pltpu.CompilerParams(vmem_limit_bytes=51 * 1024 * 1024),
        name="local",
    )(own.reshape(n_head * 8, half), mate.reshape(n_head * 8, half), halo0, halo1, w_qkv, lr_rows, taps, base)

    groups = [[2 * j + (c + j) % 2 for j in range(n_seq // 2)] for c in range(2)]
    received = lax.all_gather(send, "seq", axis_index_groups=groups)
    rows = pl.pallas_call(
        chain_kernel,
        out_shape=jax.ShapeDtypeStruct((128, 128), F32),
        in_specs=[vmem] * 4,
        out_specs=vmem,
        compiler_params=params,
        name="chain",
    )(received, qeff, oeff, w_init)
    other = lax.ppermute(rows, "seq", swap)
    partial = pl.pallas_call(
        output_kernel,
        out_shape=jax.ShapeDtypeStruct((n_head * 8, half), BF16),
        in_specs=[vmem] * 3,
        out_specs=vmem,
        compiler_params=params,
        name="output",
    )(rows, other, w_out)
    parts = lax.all_to_all(partial.reshape(n_head, 8, half), "head", 0, 0)
    return pl.pallas_call(
        total_kernel,
        out_shape=jax.ShapeDtypeStruct(tokens.shape, BF16),
        in_specs=[vmem],
        out_specs=vmem,
        scratch_shapes=[pltpu.VMEM((half // 128, 8, 128), F32)],
        compiler_params=params,
        name="total",
    )(parts)


def solution(mesh):
    placed = (
        P(("seq", "head"), None),
        P(None, "head", None),
        P("head", None),
        P("head"),
        P(None, None, "head"),
        P(None, "head", None, None),
        P("head", None),
    )
    return jax.shard_map(
        shards, mesh=mesh, in_specs=placed, out_specs=P(("seq", "head"), None), check_vma=False
    )
```

```python
import jax
import jax.numpy as jnp
from jax import lax
from jax.experimental import pallas as pl
from jax.experimental.pallas import tpu as pltpu
from jax.sharding import PartitionSpec as P

MB = 16
KERNEL = 4
EPSILON = 1e-05
F32 = jnp.float32
BF16 = jnp.bfloat16


def mm(a, b, ca=1, cb=0):
    return lax.dot_general(a, b, (((ca,), (cb,)), ((), ())), preferred_element_type=F32)


def cat(parts, axis):
    return jnp.concatenate(parts, axis=axis)


def normed(u):
    centred = u - jnp.mean(u, axis=0, keepdims=True)
    return centred * lax.rsqrt(jnp.mean(centred * centred, axis=0, keepdims=True) + EPSILON)


def role_of(place):
    return (place + place // 2) % 2


def fold_kernel(tokens_ref, out_ref, wide_ref):
    half = out_ref.shape[2]
    for j in range(half // 128):
        cols = slice(j * 128, (j + 1) * 128)
        for part in range(2):
            piece = tokens_ref[:, part * half + j * 128:part * half + (j + 1) * 128].astype(F32)
            wide_ref[j, pl.ds(part, 4, stride=2), :] = piece
        block = wide_ref[j].astype(BF16)
        for i in range(out_ref.shape[0]):
            out_ref[i, :, cols] = block


def prepare_kernel(w_hbm, lrw_ref, conv_ref, base_ref, w_ref, lrp_ref, taps_ref, rate_ref, sem):
    role = role_of(lax.axis_index("seq"))
    used = pl.ds(pl.multiple_of(64 * role, 64), 128)
    fetch = pltpu.make_async_copy(w_hbm.at[:, used, :], w_ref, sem)
    fetch.start()
    lrw = lrw_ref[...].astype(F32)
    whole = jnp.where(role == 0, lrw[0:1], lrw[2:3])
    lrp_ref[...] = cat([whole, lrw[1:2], jnp.zeros((14, lrw.shape[1]), F32)], 0).astype(BF16)
    inner = conv_ref.shape[2]
    taps_rows = cat([conv_ref[0], conv_ref[1]], 0)
    taps_ref[...] = cat([taps_rows, jnp.zeros((2 * KERNEL, 256 - inner), F32)], 1).T
    base = base_ref[...] / MB
    rate_ref[...] = jnp.zeros_like(rate_ref)
    rate_ref[0:1, :] = jnp.broadcast_to(jnp.where(role == 0, base[0:1, 0:1], base[0:1, 2:3]), (1, 128))
    rate_ref[1:2, :] = jnp.broadcast_to(base[0:1, 1:2], (1, 128))
    fetch.wait()


def spread(src_ref, wide_ref, out_ref, row):
    half = src_ref.shape[1]
    for j in range(half // 128):
        wide_ref[j] = src_ref[:, j * 128:(j + 1) * 128].astype(F32)
        for part in range(2):
            cols = slice(part * half + j * 128, part * half + (j + 1) * 128)
            out_ref[pl.ds(row, 64), cols] = wide_ref[j, pl.ds(part, 64, stride=2), :].astype(BF16)


def local_kernel(own_ref, mate_ref, halo0_ref, halo1_ref, w_ref, lrp_ref, taps_ref, rate_ref,
                 send_ref, qeff_ref, oeff_ref, wide_ref, tail_ref, xall_ref):
    place = lax.axis_index("seq")
    core = place % 2
    role = role_of(place)
    half = halo0_ref.shape[1]
    spread(own_ref, wide_ref, xall_ref, pl.multiple_of(64 * core, 64))
    spread(mate_ref, wide_ref, xall_ref, pl.multiple_of(64 * (1 - core), 64))
    halo = jnp.where(core == 0, halo0_ref[...].astype(F32), halo1_ref[...].astype(F32))
    for j in range(half // 128):
        tail_ref[j, 0:24, :] = jnp.zeros((24, 128), F32)
        tail_ref[j, 24:32, :] = halo[:, j * 128:(j + 1) * 128]
        for part in range(2):
            cols = slice(part * half + j * 128, part * half + (j + 1) * 128)
            xall_ref[240:256, cols] = tail_ref[j, pl.ds(part, 16, stride=2), :].astype(BF16)
    at = pl.multiple_of(128 * role, 64)
    whole = pl.ds(pl.multiple_of(64 * role, 64), 64)
    shared = pl.ds(pl.multiple_of(64 * (1 - role), 64), 64)
    mid = pl.ds(pl.multiple_of(64 - 32 * role, 32), 32)
    rows = cat([
        w_ref[0, whole, :], w_ref[0, shared, :], w_ref[1, whole, :], w_ref[1, shared, :],
        w_ref[2, whole, :], w_ref[2, mid, :], lrp_ref[...],
    ], 0)
    proj = mm(rows, xall_ref[...], 1, 1)
    lane = lax.broadcasted_iota(jnp.int32, (128, 128), 1)
    taps = cat([taps_ref[pl.ds(at, 64), :], taps_ref[64:128, :]], 0)
    convs = []
    for i in range(2):
        raw = proj[128 * i:128 * i + 128, 0:128].astype(BF16).astype(F32)
        edge = proj[128 * i:128 * i + 128, 128:256].astype(BF16).astype(F32)
        first = KERNEL * i
        conv = taps[:, first + KERNEL - 1:first + KERNEL] * raw
        for back in range(1, KERNEL):
            moved = jnp.where(lane < back, pltpu.roll(edge, back, 1), pltpu.roll(raw, back, 1))
            conv = conv + taps[:, first + KERNEL - 1 - back:first + KERNEL - back] * moved
        convs.append(conv)

    src = lax.broadcasted_iota(jnp.int32, (128, 128), 0)
    dst = lax.broadcasted_iota(jnp.int32, (128, 128), 1)
    strict = dst // MB > src // MB
    eye = jnp.where(src == dst, 1.0, 0.0).astype(F32)

    maps = []
    for slot in range(2):
        lo, hi = slot * 64, (slot + 1) * 64
        q = convs[0][lo:hi]
        k = convs[1][lo:hi]
        k = k * lax.rsqrt((jnp.mean(k * k, axis=0, keepdims=True) + EPSILON) * 64)
        rate = jax.nn.sigmoid(proj[352 + slot:353 + slot, 0:128]) * rate_ref[slot:slot + 1, :]
        v = proj[256:320, 0:128] if slot == 0 else proj[320:352, 0:128]
        kb = k.astype(BF16)
        kt = kb.T
        grams = mm(kt, cat([kb, q.astype(BF16)], 1))
        u = jnp.where(strict, grams[:, 0:128], 0.0) * rate
        ub = u.astype(BF16)
        u2 = mm(ub, ub)
        u2b = u2.astype(BF16)
        u4 = mm(u2b, u2b)
        t1 = eye - u + u2 - mm(ub, u2b)
        t = t1 + mm(t1.astype(BF16), u4.astype(BF16))
        rev = t.T * rate
        fwd = rev.T
        scores = grams[:, 128:256]
        seen_f = jnp.where(dst >= src, scores, 0.0).astype(BF16)
        seen_r = jnp.where(dst <= src, scores, 0.0).astype(BF16)
        solved_f = mm(fwd.astype(BF16), cat([seen_f, kt], 1)).astype(BF16)
        solved_r = mm(rev.astype(BF16), cat([seen_r, kt], 1)).astype(BF16)
        stacked = cat([kb, v.astype(BF16)], 0)
        pair = []
        for way, solved in enumerate((solved_f, solved_r)):
            both = mm(stacked, solved)
            qeff_ref[way, lo:hi, :] = (q - both[0:64, 0:128]).astype(BF16)
            oeff_ref[way, lo:lo + v.shape[0], :] = both[64:, 0:128]
            pair.append((-both[0:64, 128:192], both[64:, 128:192]))
        maps.append(pair)
    (a0, b0), (a1, b1) = maps[0][0], maps[1][0]
    send_ref[0:64, :] = cat([a0, a1], 1).astype(BF16)
    for way in range(2):
        b0, b1 = maps[0][way][1], maps[1][way][1]
        packed = cat([b0[0:48], cat([b0[48:64], b1], 0)], 1)
        send_ref[64 + 48 * way:112 + 48 * way, :] = packed.astype(BF16)


def chain_kernel(maps_ref, qeff_ref, oeff_ref, init_ref, out_ref):
    place = lax.axis_index("seq")
    role = role_of(place)
    chip = place // 2
    chips = maps_ref.shape[0]
    states = []
    for way in range(2):
        shared = init_ref[way, 1, pl.ds(pl.multiple_of(32 * role, 32), 32), :]
        states.append([init_ref[way, 2 * role], shared])
    for i in range(chips - 1):
        for way in range(2):
            j = i if way == 0 else chips - 1 - i
            live = (j < chip) if way == 0 else (j > chip)
            block = maps_ref[j]
            whole, shared = states[way]
            at = 64 + 48 * way
            b0 = cat([block[at:at + 48, 0:64], block[at:at + 16, 64:128]], 0).astype(F32)
            b1 = block[at + 16:at + 48, 64:128].astype(F32)
            new0 = whole + mm(whole.astype(BF16), block[0:64, 0:64], 1, way) + b0
            new1 = shared + mm(shared.astype(BF16), block[0:64, 64:128], 1, way) + b1
            states[way] = [jnp.where(live, new0, whole), jnp.where(live, new1, shared)]
    sums = None
    for way in range(2):
        whole = mm(states[way][0].astype(BF16), qeff_ref[way, 0:64, :]) + oeff_ref[way, 0:64, :]
        sums = normed(whole) if sums is None else sums + normed(whole)
        shared = mm(states[way][1].astype(BF16), qeff_ref[way, 64:128, :]) + oeff_ref[way, 64:96, :]
        out_ref[64 + 32 * way:96 + 32 * way, :] = shared
    out_ref[0:64, :] = sums


def output_kernel(mine_ref, mate_ref, w_ref, out_ref):
    place = lax.axis_index("seq")
    core = place % 2
    role = role_of(place)
    mine = mine_ref[...]
    mate = mate_ref[...]
    low = jnp.where(role == 0, mine, mate)
    high = jnp.where(role == 0, mate, mine)
    middle = normed(cat([low[64:96], high[64:96]], 0)) + normed(cat([low[96:128], high[96:128]], 0))
    hidden = cat([low[0:64], middle, high[0:64]], 0).astype(BF16)
    row = lax.broadcasted_iota(jnp.int32, (128, 128), 0)
    col = lax.broadcasted_iota(jnp.int32, (128, 128), 1)
    pick = jnp.where(col == row // 2 + 64 * core, 1.0, 0.0).astype(BF16)
    twice = mm(pick, hidden, 1, 1).astype(BF16)
    half = out_ref.shape[1]
    even = lax.broadcasted_iota(jnp.int32, (128, half), 0) % 2 == 0
    first = mm(twice, w_ref[:, 0:half])
    second = mm(twice, w_ref[:, half:2 * half])
    out_ref[...] = jnp.where(even, first, second).astype(BF16)


def total_kernel(parts_ref, out_ref, wide_ref):
    acc = parts_ref[0].astype(F32)
    for i in range(1, parts_ref.shape[0]):
        acc = acc + parts_ref[i].astype(F32)
    half = acc.shape[1]
    for j in range(half // 128):
        wide_ref[j] = acc[:, j * 128:(j + 1) * 128]
        for part in range(2):
            out_ref[:, part * half + j * 128:part * half + (j + 1) * 128] = (
                wide_ref[j, pl.ds(part, 4, stride=2), :].astype(BF16))


def shards(tokens, w_qkv, lr_weight, lr_base, conv_weight, w_init, w_out):
    width = tokens.shape[1]
    half = width // 2
    inner = w_qkv.shape[1]
    n_seq = lax.axis_size("seq")
    n_head = lax.axis_size("head")
    params = pltpu.CompilerParams(vmem_limit_bytes=24 * 1024 * 1024)
    vmem = pl.BlockSpec(memory_space=pltpu.VMEM)
    hbm = pl.BlockSpec(memory_space=pl.ANY)

    folded = pl.pallas_call(
        fold_kernel,
        out_shape=jax.ShapeDtypeStruct((n_head, 8, half), BF16),
        in_specs=[vmem],
        out_specs=vmem,
        scratch_shapes=[pltpu.VMEM((half // 128, 8, 128), F32)],
        compiler_params=params,
        name="fold",
    )(tokens)
    own = lax.all_to_all(folded, "head", 0, 0)
    weights, lr_rows, taps, base = pl.pallas_call(
        prepare_kernel,
        out_shape=(
            jax.ShapeDtypeStruct((3, 128, width), BF16),
            jax.ShapeDtypeStruct((16, width), BF16),
            jax.ShapeDtypeStruct((256, 2 * KERNEL), F32),
            jax.ShapeDtypeStruct((8, 128), F32),
        ),
        in_specs=[hbm] + [vmem] * 3,
        out_specs=(vmem,) * 4,
        scratch_shapes=[pltpu.SemaphoreType.DMA(())],
        compiler_params=params,
        name="prepare",
    )(w_qkv, lr_weight, conv_weight, lr_base.reshape(1, lr_base.shape[0]))
    own, weights = lax.optimization_barrier((own, weights))
    swap = [(i, i ^ 1) for i in range(n_seq)]
    mate = lax.ppermute(own, "seq", swap)
    tail = own[n_head - 1]
    halo0 = lax.ppermute(tail, "seq", [(i, i + 1) for i in range(1, n_seq - 1, 2)])
    halo1 = lax.ppermute(tail, "seq", [(i, i + 2) for i in range(1, n_seq - 2, 2)])
    send, qeff, oeff = pl.pallas_call(
        local_kernel,
        out_shape=(
            jax.ShapeDtypeStruct((160, 128), BF16),
            jax.ShapeDtypeStruct((2, 128, 128), BF16),
            jax.ShapeDtypeStruct((2, 96, 128), F32),
        ),
        in_specs=[vmem] * 8,
        out_specs=(vmem, vmem, vmem),
        scratch_shapes=[
            pltpu.VMEM((half // 128, 128, 128), F32),
            pltpu.VMEM((half // 128, 32, 128), F32),
            pltpu.VMEM((256, width), BF16),
        ],
        compiler_params=params,
        name="local",
    )(own.reshape(n_head * 8, half), mate.reshape(n_head * 8, half), halo0, halo1, weights, lr_rows, taps, base)

    groups = [[2 * j + (c + j) % 2 for j in range(n_seq // 2)] for c in range(2)]
    received = lax.all_gather(send, "seq", axis_index_groups=groups)
    rows = pl.pallas_call(
        chain_kernel,
        out_shape=jax.ShapeDtypeStruct((128, 128), F32),
        in_specs=[vmem] * 4,
        out_specs=vmem,
        compiler_params=params,
        name="chain",
    )(received, qeff, oeff, w_init)
    other = lax.ppermute(rows, "seq", swap)
    partial = pl.pallas_call(
        output_kernel,
        out_shape=jax.ShapeDtypeStruct((n_head * 8, half), BF16),
        in_specs=[vmem] * 3,
        out_specs=vmem,
        compiler_params=params,
        name="output",
    )(rows, other, w_out)
    parts = lax.all_to_all(partial.reshape(n_head, 8, half), "head", 0, 0)
    return pl.pallas_call(
        total_kernel,
        out_shape=jax.ShapeDtypeStruct(tokens.shape, BF16),
        in_specs=[vmem],
        out_specs=vmem,
        scratch_shapes=[pltpu.VMEM((half // 128, 8, 128), F32)],
        compiler_params=params,
        name="total",
    )(parts)


def solution(mesh):
    placed = (
        P(("seq", "head"), None),
        P(None, "head", None),
        P("head", None),
        P("head"),
        P(None, None, "head"),
        P(None, "head", None, None),
        P("head", None),
    )
    return jax.shard_map(
        shards, mesh=mesh, in_specs=placed, out_specs=P(("seq", "head"), None), check_vma=False
    )
```

```python
import jax
import jax.numpy as jnp
from jax import lax
from jax.experimental import pallas as pl
from jax.experimental.pallas import tpu as pltpu
from jax.sharding import PartitionSpec as P

MB = 16
KERNEL = 4
EPSILON = 1e-05
F32 = jnp.float32
BF16 = jnp.bfloat16


def mm(a, b, ca=1, cb=0):
    return lax.dot_general(a, b, (((ca,), (cb,)), ((), ())), preferred_element_type=F32)


def cat(parts, axis):
    return jnp.concatenate(parts, axis=axis)


def normed(u):
    centred = u - jnp.mean(u, axis=0, keepdims=True)
    return centred * lax.rsqrt(jnp.mean(centred * centred, axis=0, keepdims=True) + EPSILON)


def role_of(place):
    return (place + place // 2) % 2


def fold_kernel(tokens_ref, out_ref, wide_ref):
    half = out_ref.shape[2]
    for j in range(half // 128):
        cols = slice(j * 128, (j + 1) * 128)
        for part in range(2):
            piece = tokens_ref[:, part * half + j * 128:part * half + (j + 1) * 128].astype(F32)
            wide_ref[j, pl.ds(part, 4, stride=2), :] = piece
        block = wide_ref[j].astype(BF16)
        for i in range(out_ref.shape[0]):
            out_ref[i, :, cols] = block


def prepare_kernel(w_hbm, lrw_ref, conv_ref, base_ref, w_ref, lrp_ref, taps_ref, rate_ref, sem):
    role = role_of(lax.axis_index("seq"))
    used = pl.ds(pl.multiple_of(64 * role, 64), 128)
    fetch = pltpu.make_async_copy(w_hbm.at[:, used, :], w_ref, sem)
    fetch.start()
    lrw = lrw_ref[...].astype(F32)
    whole = jnp.where(role == 0, lrw[0:1], lrw[2:3])
    lrp_ref[...] = cat([whole, lrw[1:2], jnp.zeros((14, lrw.shape[1]), F32)], 0).astype(BF16)
    inner = conv_ref.shape[2]
    taps_rows = cat([conv_ref[0], conv_ref[1]], 0)
    taps_ref[...] = cat([taps_rows, jnp.zeros((2 * KERNEL, 256 - inner), F32)], 1).T
    base = base_ref[...] / MB
    rate_ref[...] = jnp.zeros_like(rate_ref)
    rate_ref[0:1, :] = jnp.broadcast_to(jnp.where(role == 0, base[0:1, 0:1], base[0:1, 2:3]), (1, 128))
    rate_ref[1:2, :] = jnp.broadcast_to(base[0:1, 1:2], (1, 128))
    fetch.wait()


def spread(src_ref, wide_ref, out_ref, row):
    half = src_ref.shape[1]
    for j in range(half // 128):
        wide_ref[j] = src_ref[:, j * 128:(j + 1) * 128].astype(F32)
        for part in range(2):
            cols = slice(part * half + j * 128, part * half + (j + 1) * 128)
            out_ref[pl.ds(row, 64), cols] = wide_ref[j, pl.ds(part, 64, stride=2), :].astype(BF16)


def local_kernel(own_ref, mate_ref, halo0_ref, halo1_ref, w_ref, lrp_ref, taps_ref, rate_ref,
                 send_ref, qeff_ref, oeff_ref, wide_ref, tail_ref, xall_ref):
    place = lax.axis_index("seq")
    core = place % 2
    role = role_of(place)
    half = halo0_ref.shape[1]
    spread(own_ref, wide_ref, xall_ref, pl.multiple_of(64 * core, 64))
    spread(mate_ref, wide_ref, xall_ref, pl.multiple_of(64 * (1 - core), 64))
    halo = jnp.where(core == 0, halo0_ref[...].astype(F32), halo1_ref[...].astype(F32))
    for j in range(half // 128):
        tail_ref[j, 0:24, :] = jnp.zeros((24, 128), F32)
        tail_ref[j, 24:32, :] = halo[:, j * 128:(j + 1) * 128]
        for part in range(2):
            cols = slice(part * half + j * 128, part * half + (j + 1) * 128)
            xall_ref[240:256, cols] = tail_ref[j, pl.ds(part, 16, stride=2), :].astype(BF16)
    at = pl.multiple_of(128 * role, 64)
    whole = pl.ds(pl.multiple_of(64 * role, 64), 64)
    shared = pl.ds(pl.multiple_of(64 * (1 - role), 64), 64)
    mid = pl.ds(pl.multiple_of(64 - 32 * role, 32), 32)
    rows = cat([
        w_ref[0, whole, :], w_ref[0, shared, :], w_ref[1, whole, :], w_ref[1, shared, :],
        w_ref[2, whole, :], w_ref[2, mid, :], lrp_ref[...],
    ], 0)
    proj = mm(rows, xall_ref[...], 1, 1)
    lane = lax.broadcasted_iota(jnp.int32, (128, 128), 1)
    taps = cat([taps_ref[pl.ds(at, 64), :], taps_ref[64:128, :]], 0)
    convs = []
    for i in range(2):
        raw = proj[128 * i:128 * i + 128, 0:128].astype(BF16).astype(F32)
        edge = proj[128 * i:128 * i + 128, 128:256].astype(BF16).astype(F32)
        first = KERNEL * i
        conv = taps[:, first + KERNEL - 1:first + KERNEL] * raw
        for back in range(1, KERNEL):
            moved = jnp.where(lane < back, pltpu.roll(edge, back, 1), pltpu.roll(raw, back, 1))
            conv = conv + taps[:, first + KERNEL - 1 - back:first + KERNEL - back] * moved
        convs.append(conv)

    src = lax.broadcasted_iota(jnp.int32, (128, 128), 0)
    dst = lax.broadcasted_iota(jnp.int32, (128, 128), 1)
    strict = dst // MB > src // MB
    eye = jnp.where(src == dst, 1.0, 0.0).astype(F32)

    two = range(2)
    q = [convs[0][64 * i:64 * i + 64] for i in two]
    k = [convs[1][64 * i:64 * i + 64] for i in two]
    k = [x * lax.rsqrt((jnp.mean(x * x, axis=0, keepdims=True) + EPSILON) * 64) for x in k]
    rate = [jax.nn.sigmoid(proj[352 + i:353 + i, 0:128]) * rate_ref[i:i + 1, :] for i in two]
    v = [proj[256:320, 0:128], proj[320:352, 0:128]]
    kb = [x.astype(BF16) for x in k]
    kt = [x.T for x in kb]
    grams = [mm(kt[i], cat([kb[i], q[i].astype(BF16)], 1)) for i in two]
    u = [jnp.where(strict, grams[i][:, 0:128], 0.0) * rate[i] for i in two]
    ub = [x.astype(BF16) for x in u]
    u2 = [mm(x, x) for x in ub]
    u2b = [x.astype(BF16) for x in u2]
    u4 = [mm(x, x).astype(BF16) for x in u2b]
    u3 = [mm(ub[i], u2b[i]) for i in two]
    t1 = [eye - u[i] + u2[i] - u3[i] for i in two]
    t = [t1[i] + mm(t1[i].astype(BF16), u4[i]) for i in two]
    rev = [t[i].T * rate[i] for i in two]
    ways = [[x.T.astype(BF16) for x in rev], [x.astype(BF16) for x in rev]]
    seen = [[jnp.where(mask, grams[i][:, 128:256], 0.0).astype(BF16) for i in two] for mask in (dst >= src, dst <= src)]
    solved = [[mm(ways[w][i], cat([seen[w][i], kt[i]], 1)).astype(BF16) for i in two] for w in two]
    stacked = [cat([kb[i], v[i].astype(BF16)], 0) for i in two]
    both = [[mm(stacked[i], solved[w][i]) for i in two] for w in two]
    for w in two:
        for i in two:
            qeff_ref[w, 64 * i:64 * i + 64, :] = (q[i] - both[w][i][0:64, 0:128]).astype(BF16)
            oeff_ref[w, 64 * i:64 * i + v[i].shape[0], :] = both[w][i][64:, 0:128]
    maps = [[(-both[w][i][0:64, 128:192], both[w][i][64:, 128:192]) for w in two] for i in two]
    (a0, b0), (a1, b1) = maps[0][0], maps[1][0]
    send_ref[0:64, :] = cat([a0, a1], 1).astype(BF16)
    for way in range(2):
        b0, b1 = maps[0][way][1], maps[1][way][1]
        packed = cat([b0[0:48], cat([b0[48:64], b1], 0)], 1)
        send_ref[64 + 48 * way:112 + 48 * way, :] = packed.astype(BF16)


def chain_kernel(maps_ref, qeff_ref, oeff_ref, init_ref, out_ref):
    place = lax.axis_index("seq")
    role = role_of(place)
    chip = place // 2
    chips = maps_ref.shape[0]
    states = []
    for way in range(2):
        shared = init_ref[way, 1, pl.ds(pl.multiple_of(32 * role, 32), 32), :]
        states.append([init_ref[way, 2 * role], shared])
    for i in range(chips - 1):
        for way in range(2):
            j = i if way == 0 else chips - 1 - i
            live = (j < chip) if way == 0 else (j > chip)
            block = maps_ref[j]
            whole, shared = states[way]
            at = 64 + 48 * way
            b0 = cat([block[at:at + 48, 0:64], block[at:at + 16, 64:128]], 0).astype(F32)
            b1 = block[at + 16:at + 48, 64:128].astype(F32)
            new0 = whole + mm(whole.astype(BF16), block[0:64, 0:64], 1, way) + b0
            new1 = shared + mm(shared.astype(BF16), block[0:64, 64:128], 1, way) + b1
            states[way] = [jnp.where(live, new0, whole), jnp.where(live, new1, shared)]
    sums = None
    for way in range(2):
        whole = mm(states[way][0].astype(BF16), qeff_ref[way, 0:64, :]) + oeff_ref[way, 0:64, :]
        sums = normed(whole) if sums is None else sums + normed(whole)
        shared = mm(states[way][1].astype(BF16), qeff_ref[way, 64:128, :]) + oeff_ref[way, 64:96, :]
        out_ref[64 + 32 * way:96 + 32 * way, :] = shared
    out_ref[0:64, :] = sums


def output_kernel(mine_ref, mate_ref, w_ref, out_ref):
    place = lax.axis_index("seq")
    core = place % 2
    role = role_of(place)
    mine = mine_ref[...]
    mate = mate_ref[...]
    low = jnp.where(role == 0, mine, mate)
    high = jnp.where(role == 0, mate, mine)
    middle = normed(cat([low[64:96], high[64:96]], 0)) + normed(cat([low[96:128], high[96:128]], 0))
    hidden = cat([low[0:64], middle, high[0:64]], 0).astype(BF16)
    row = lax.broadcasted_iota(jnp.int32, (128, 128), 0)
    col = lax.broadcasted_iota(jnp.int32, (128, 128), 1)
    pick = jnp.where(col == row // 2 + 64 * core, 1.0, 0.0).astype(BF16)
    twice = mm(pick, hidden, 1, 1).astype(BF16)
    half = out_ref.shape[1]
    even = lax.broadcasted_iota(jnp.int32, (128, half), 0) % 2 == 0
    first = mm(twice, w_ref[:, 0:half])
    second = mm(twice, w_ref[:, half:2 * half])
    out_ref[...] = jnp.where(even, first, second).astype(BF16)


def total_kernel(parts_ref, out_ref, wide_ref):
    acc = parts_ref[0].astype(F32)
    for i in range(1, parts_ref.shape[0]):
        acc = acc + parts_ref[i].astype(F32)
    half = acc.shape[1]
    for j in range(half // 128):
        wide_ref[j] = acc[:, j * 128:(j + 1) * 128]
        for part in range(2):
            out_ref[:, part * half + j * 128:part * half + (j + 1) * 128] = (
                wide_ref[j, pl.ds(part, 4, stride=2), :].astype(BF16))


def shards(tokens, w_qkv, lr_weight, lr_base, conv_weight, w_init, w_out):
    width = tokens.shape[1]
    half = width // 2
    inner = w_qkv.shape[1]
    n_seq = lax.axis_size("seq")
    n_head = lax.axis_size("head")
    params = pltpu.CompilerParams(vmem_limit_bytes=24 * 1024 * 1024)
    vmem = pl.BlockSpec(memory_space=pltpu.VMEM)
    hbm = pl.BlockSpec(memory_space=pl.ANY)

    folded = pl.pallas_call(
        fold_kernel,
        out_shape=jax.ShapeDtypeStruct((n_head, 8, half), BF16),
        in_specs=[vmem],
        out_specs=vmem,
        scratch_shapes=[pltpu.VMEM((half // 128, 8, 128), F32)],
        compiler_params=params,
        name="fold",
    )(tokens)
    own = lax.all_to_all(folded, "head", 0, 0)
    weights, lr_rows, taps, base = pl.pallas_call(
        prepare_kernel,
        out_shape=(
            jax.ShapeDtypeStruct((3, 128, width), BF16),
            jax.ShapeDtypeStruct((16, width), BF16),
            jax.ShapeDtypeStruct((256, 2 * KERNEL), F32),
            jax.ShapeDtypeStruct((8, 128), F32),
        ),
        in_specs=[hbm] + [vmem] * 3,
        out_specs=(vmem,) * 4,
        scratch_shapes=[pltpu.SemaphoreType.DMA(())],
        compiler_params=params,
        name="prepare",
    )(w_qkv, lr_weight, conv_weight, lr_base.reshape(1, lr_base.shape[0]))
    own, weights = lax.optimization_barrier((own, weights))
    swap = [(i, i ^ 1) for i in range(n_seq)]
    mate = lax.ppermute(own, "seq", swap)
    tail = own[n_head - 1]
    halo0 = lax.ppermute(tail, "seq", [(i, i + 1) for i in range(1, n_seq - 1, 2)])
    halo1 = lax.ppermute(tail, "seq", [(i, i + 2) for i in range(1, n_seq - 2, 2)])
    send, qeff, oeff = pl.pallas_call(
        local_kernel,
        out_shape=(
            jax.ShapeDtypeStruct((160, 128), BF16),
            jax.ShapeDtypeStruct((2, 128, 128), BF16),
            jax.ShapeDtypeStruct((2, 96, 128), F32),
        ),
        in_specs=[vmem] * 8,
        out_specs=(vmem, vmem, vmem),
        scratch_shapes=[
            pltpu.VMEM((half // 128, 128, 128), F32),
            pltpu.VMEM((half // 128, 32, 128), F32),
            pltpu.VMEM((256, width), BF16),
        ],
        compiler_params=params,
        name="local",
    )(own.reshape(n_head * 8, half), mate.reshape(n_head * 8, half), halo0, halo1, weights, lr_rows, taps, base)

    groups = [[2 * j + (c + j) % 2 for j in range(n_seq // 2)] for c in range(2)]
    received = lax.all_gather(send, "seq", axis_index_groups=groups)
    rows = pl.pallas_call(
        chain_kernel,
        out_shape=jax.ShapeDtypeStruct((128, 128), F32),
        in_specs=[vmem] * 4,
        out_specs=vmem,
        compiler_params=params,
        name="chain",
    )(received, qeff, oeff, w_init)
    other = lax.ppermute(rows, "seq", swap)
    partial = pl.pallas_call(
        output_kernel,
        out_shape=jax.ShapeDtypeStruct((n_head * 8, half), BF16),
        in_specs=[vmem] * 3,
        out_specs=vmem,
        compiler_params=params,
        name="output",
    )(rows, other, w_out)
    parts = lax.all_to_all(partial.reshape(n_head, 8, half), "head", 0, 0)
    return pl.pallas_call(
        total_kernel,
        out_shape=jax.ShapeDtypeStruct(tokens.shape, BF16),
        in_specs=[vmem],
        out_specs=vmem,
        scratch_shapes=[pltpu.VMEM((half // 128, 8, 128), F32)],
        compiler_params=params,
        name="total",
    )(parts)


def solution(mesh):
    placed = (
        P(("seq", "head"), None),
        P(None, "head", None),
        P("head", None),
        P("head"),
        P(None, None, "head"),
        P(None, "head", None, None),
        P("head", None),
    )
    return jax.shard_map(
        shards, mesh=mesh, in_specs=placed, out_specs=P(("seq", "head"), None), check_vma=False
    )
```

```python
import jax
import jax.numpy as jnp
from jax import lax
from jax.experimental import pallas as pl
from jax.experimental.pallas import tpu as pltpu
from jax.sharding import PartitionSpec as P

MB = 16
KERNEL = 4
EPSILON = 1e-05
F32 = jnp.float32
BF16 = jnp.bfloat16


def mm(a, b, ca=1, cb=0):
    return lax.dot_general(a, b, (((ca,), (cb,)), ((), ())), preferred_element_type=F32)


def cat(parts, axis):
    return jnp.concatenate(parts, axis=axis)


def normed(u):
    centred = u - jnp.mean(u, axis=0, keepdims=True)
    return centred * lax.rsqrt(jnp.mean(centred * centred, axis=0, keepdims=True) + EPSILON)


def role_of(place):
    return (place + place // 2) % 2


def fold_kernel(tokens_ref, out_ref, wide_ref):
    half = out_ref.shape[2]
    for j in range(half // 128):
        cols = slice(j * 128, (j + 1) * 128)
        for part in range(2):
            piece = tokens_ref[:, part * half + j * 128:part * half + (j + 1) * 128].astype(F32)
            wide_ref[j, pl.ds(part, 4, stride=2), :] = piece
        block = wide_ref[j].astype(BF16)
        for i in range(out_ref.shape[0]):
            out_ref[i, :, cols] = block


def prepare_kernel(w_hbm, lrw_ref, conv_ref, base_ref, w_ref, lrp_ref, taps_ref, rate_ref, sem):
    role = role_of(lax.axis_index("seq"))
    used = pl.ds(pl.multiple_of(64 * role, 64), 128)
    fetch = pltpu.make_async_copy(w_hbm.at[:, used, :], w_ref, sem)
    fetch.start()
    lrw = lrw_ref[...].astype(F32)
    whole = jnp.where(role == 0, lrw[0:1], lrw[2:3])
    lrp_ref[...] = cat([whole, lrw[1:2], jnp.zeros((14, lrw.shape[1]), F32)], 0).astype(BF16)
    inner = conv_ref.shape[2]
    taps_rows = cat([conv_ref[0], conv_ref[1]], 0)
    taps_ref[...] = cat([taps_rows, jnp.zeros((2 * KERNEL, 256 - inner), F32)], 1).T
    base = base_ref[...] / MB
    rate_ref[...] = jnp.zeros_like(rate_ref)
    rate_ref[0:1, :] = jnp.broadcast_to(jnp.where(role == 0, base[0:1, 0:1], base[0:1, 2:3]), (1, 128))
    rate_ref[1:2, :] = jnp.broadcast_to(base[0:1, 1:2], (1, 128))
    fetch.wait()


def spread(src_ref, wide_ref, out_ref, row):
    half = src_ref.shape[1]
    for j in range(half // 128):
        wide_ref[j] = src_ref[:, j * 128:(j + 1) * 128].astype(F32)
        for part in range(2):
            cols = slice(part * half + j * 128, part * half + (j + 1) * 128)
            out_ref[pl.ds(row, 64), cols] = wide_ref[j, pl.ds(part, 64, stride=2), :].astype(BF16)


def tail_kernel(halo0_ref, halo1_ref, out_ref, wide_ref):
    core = lax.axis_index("seq") % 2
    half = halo0_ref.shape[1]
    halo = jnp.where(core == 0, halo0_ref[...].astype(F32), halo1_ref[...].astype(F32))
    for j in range(half // 128):
        wide_ref[j, 0:24, :] = jnp.zeros((24, 128), F32)
        wide_ref[j, 24:32, :] = halo[:, j * 128:(j + 1) * 128]
        for part in range(2):
            cols = slice(part * half + j * 128, part * half + (j + 1) * 128)
            out_ref[:, cols] = wide_ref[j, pl.ds(part, 16, stride=2), :].astype(BF16)


def local_kernel(own_ref, mate_ref, tail_ref, w_ref, lrp_ref, taps_ref, rate_ref,
                 send_ref, qeff_ref, oeff_ref, wide_ref, xall_ref):
    place = lax.axis_index("seq")
    core = place % 2
    role = role_of(place)
    spread(own_ref, wide_ref, xall_ref, pl.multiple_of(64 * core, 64))
    spread(mate_ref, wide_ref, xall_ref, pl.multiple_of(64 * (1 - core), 64))
    xall_ref[240:256, :] = tail_ref[...]
    at = pl.multiple_of(128 * role, 64)
    whole = pl.ds(pl.multiple_of(64 * role, 64), 64)
    shared = pl.ds(pl.multiple_of(64 * (1 - role), 64), 64)
    mid = pl.ds(pl.multiple_of(64 - 32 * role, 32), 32)
    rows = cat([
        w_ref[0, whole, :], w_ref[0, shared, :], w_ref[1, whole, :], w_ref[1, shared, :],
        w_ref[2, whole, :], w_ref[2, mid, :], lrp_ref[...],
    ], 0)
    proj = mm(rows, xall_ref[...], 1, 1)
    lane = lax.broadcasted_iota(jnp.int32, (128, 128), 1)
    taps = cat([taps_ref[pl.ds(at, 64), :], taps_ref[64:128, :]], 0)
    convs = []
    for i in range(2):
        raw = proj[128 * i:128 * i + 128, 0:128].astype(BF16).astype(F32)
        edge = proj[128 * i:128 * i + 128, 128:256].astype(BF16).astype(F32)
        first = KERNEL * i
        conv = taps[:, first + KERNEL - 1:first + KERNEL] * raw
        for back in range(1, KERNEL):
            moved = jnp.where(lane < back, pltpu.roll(edge, back, 1), pltpu.roll(raw, back, 1))
            conv = conv + taps[:, first + KERNEL - 1 - back:first + KERNEL - back] * moved
        convs.append(conv)

    src = lax.broadcasted_iota(jnp.int32, (128, 128), 0)
    dst = lax.broadcasted_iota(jnp.int32, (128, 128), 1)
    strict = dst // MB > src // MB
    eye = jnp.where(src == dst, 1.0, 0.0).astype(F32)

    two = range(2)
    q = [convs[0][64 * i:64 * i + 64] for i in two]
    k = [convs[1][64 * i:64 * i + 64] for i in two]
    k = [x * lax.rsqrt((jnp.mean(x * x, axis=0, keepdims=True) + EPSILON) * 64) for x in k]
    rate = [jax.nn.sigmoid(proj[352 + i:353 + i, 0:128]) * rate_ref[i:i + 1, :] for i in two]
    v = [proj[256:320, 0:128], proj[320:352, 0:128]]
    kb = [x.astype(BF16) for x in k]
    kt = [x.T for x in kb]
    grams = [mm(kt[i], cat([kb[i], q[i].astype(BF16)], 1)) for i in two]
    u = [jnp.where(strict, grams[i][:, 0:128], 0.0) * rate[i] for i in two]
    ub = [x.astype(BF16) for x in u]
    u2 = [mm(x, x) for x in ub]
    u2b = [x.astype(BF16) for x in u2]
    u4 = [mm(x, x).astype(BF16) for x in u2b]
    u3 = [mm(ub[i], u2b[i]) for i in two]
    t1 = [eye - u[i] + u2[i] - u3[i] for i in two]
    t = [t1[i] + mm(t1[i].astype(BF16), u4[i]) for i in two]
    rev = [t[i].T * rate[i] for i in two]
    ways = [[x.T.astype(BF16) for x in rev], [x.astype(BF16) for x in rev]]
    seen = [[jnp.where(mask, grams[i][:, 128:256], 0.0).astype(BF16) for i in two] for mask in (dst >= src, dst <= src)]
    solved = [[mm(ways[w][i], cat([seen[w][i], kt[i]], 1)).astype(BF16) for i in two] for w in two]
    stacked = [cat([kb[i], v[i].astype(BF16)], 0) for i in two]
    both = [[mm(stacked[i], solved[w][i]) for i in two] for w in two]
    for w in two:
        for i in two:
            qeff_ref[w, 64 * i:64 * i + 64, :] = (q[i] - both[w][i][0:64, 0:128]).astype(BF16)
            oeff_ref[w, 64 * i:64 * i + v[i].shape[0], :] = both[w][i][64:, 0:128]
    maps = [[(-both[w][i][0:64, 128:192], both[w][i][64:, 128:192]) for w in two] for i in two]
    (a0, b0), (a1, b1) = maps[0][0], maps[1][0]
    send_ref[0:64, :] = cat([a0, a1], 1).astype(BF16)
    for way in range(2):
        b0, b1 = maps[0][way][1], maps[1][way][1]
        packed = cat([b0[0:48], cat([b0[48:64], b1], 0)], 1)
        send_ref[64 + 48 * way:112 + 48 * way, :] = packed.astype(BF16)


def chain_kernel(maps_ref, qeff_ref, oeff_ref, init_ref, out_ref):
    place = lax.axis_index("seq")
    role = role_of(place)
    chip = place // 2
    chips = maps_ref.shape[0]
    states = []
    for way in range(2):
        shared = init_ref[way, 1, pl.ds(pl.multiple_of(32 * role, 32), 32), :]
        states.append([init_ref[way, 2 * role], shared])
    for i in range(chips - 1):
        for way in range(2):
            j = i if way == 0 else chips - 1 - i
            live = (j < chip) if way == 0 else (j > chip)
            block = maps_ref[j]
            whole, shared = states[way]
            at = 64 + 48 * way
            b0 = cat([block[at:at + 48, 0:64], block[at:at + 16, 64:128]], 0).astype(F32)
            b1 = block[at + 16:at + 48, 64:128].astype(F32)
            new0 = whole + mm(whole.astype(BF16), block[0:64, 0:64], 1, way) + b0
            new1 = shared + mm(shared.astype(BF16), block[0:64, 64:128], 1, way) + b1
            states[way] = [jnp.where(live, new0, whole), jnp.where(live, new1, shared)]
    sums = None
    for way in range(2):
        whole = mm(states[way][0].astype(BF16), qeff_ref[way, 0:64, :]) + oeff_ref[way, 0:64, :]
        sums = normed(whole) if sums is None else sums + normed(whole)
        shared = mm(states[way][1].astype(BF16), qeff_ref[way, 64:128, :]) + oeff_ref[way, 64:96, :]
        out_ref[64 + 32 * way:96 + 32 * way, :] = shared
    out_ref[0:64, :] = sums


def output_kernel(mine_ref, mate_ref, w_ref, out_ref):
    place = lax.axis_index("seq")
    core = place % 2
    role = role_of(place)
    mine = mine_ref[...]
    mate = mate_ref[...]
    low = jnp.where(role == 0, mine, mate)
    high = jnp.where(role == 0, mate, mine)
    middle = normed(cat([low[64:96], high[64:96]], 0)) + normed(cat([low[96:128], high[96:128]], 0))
    hidden = cat([low[0:64], middle, high[0:64]], 0).astype(BF16)
    row = lax.broadcasted_iota(jnp.int32, (128, 128), 0)
    col = lax.broadcasted_iota(jnp.int32, (128, 128), 1)
    pick = jnp.where(col == row // 2 + 64 * core, 1.0, 0.0).astype(BF16)
    twice = mm(pick, hidden, 1, 1).astype(BF16)
    half = out_ref.shape[1]
    even = lax.broadcasted_iota(jnp.int32, (128, half), 0) % 2 == 0
    first = mm(twice, w_ref[:, 0:half])
    second = mm(twice, w_ref[:, half:2 * half])
    out_ref[...] = jnp.where(even, first, second).astype(BF16)


def total_kernel(parts_ref, out_ref, wide_ref):
    acc = parts_ref[0].astype(F32)
    for i in range(1, parts_ref.shape[0]):
        acc = acc + parts_ref[i].astype(F32)
    half = acc.shape[1]
    for j in range(half // 128):
        wide_ref[j] = acc[:, j * 128:(j + 1) * 128]
        for part in range(2):
            out_ref[:, part * half + j * 128:part * half + (j + 1) * 128] = (
                wide_ref[j, pl.ds(part, 4, stride=2), :].astype(BF16))


def shards(tokens, w_qkv, lr_weight, lr_base, conv_weight, w_init, w_out):
    width = tokens.shape[1]
    half = width // 2
    inner = w_qkv.shape[1]
    n_seq = lax.axis_size("seq")
    n_head = lax.axis_size("head")
    params = pltpu.CompilerParams(vmem_limit_bytes=24 * 1024 * 1024)
    vmem = pl.BlockSpec(memory_space=pltpu.VMEM)
    hbm = pl.BlockSpec(memory_space=pl.ANY)

    folded = pl.pallas_call(
        fold_kernel,
        out_shape=jax.ShapeDtypeStruct((n_head, 8, half), BF16),
        in_specs=[vmem],
        out_specs=vmem,
        scratch_shapes=[pltpu.VMEM((half // 128, 8, 128), F32)],
        compiler_params=params,
        name="fold",
    )(tokens)
    own = lax.all_to_all(folded, "head", 0, 0)
    weights, lr_rows, taps, base = pl.pallas_call(
        prepare_kernel,
        out_shape=(
            jax.ShapeDtypeStruct((3, 128, width), BF16),
            jax.ShapeDtypeStruct((16, width), BF16),
            jax.ShapeDtypeStruct((256, 2 * KERNEL), F32),
            jax.ShapeDtypeStruct((8, 128), F32),
        ),
        in_specs=[hbm] + [vmem] * 3,
        out_specs=(vmem,) * 4,
        scratch_shapes=[pltpu.SemaphoreType.DMA(())],
        compiler_params=params,
        name="prepare",
    )(w_qkv, lr_weight, conv_weight, lr_base.reshape(1, lr_base.shape[0]))
    own, weights = lax.optimization_barrier((own, weights))
    swap = [(i, i ^ 1) for i in range(n_seq)]
    mate = lax.ppermute(own, "seq", swap)
    tail = own[n_head - 1]
    halo0 = lax.ppermute(tail, "seq", [(i, i + 1) for i in range(1, n_seq - 1, 2)])
    halo1 = lax.ppermute(tail, "seq", [(i, i + 2) for i in range(1, n_seq - 2, 2)])
    tails = pl.pallas_call(
        tail_kernel,
        out_shape=jax.ShapeDtypeStruct((16, width), BF16),
        in_specs=[vmem] * 2,
        out_specs=vmem,
        scratch_shapes=[pltpu.VMEM((half // 128, 32, 128), F32)],
        compiler_params=params,
        cost_estimate=pl.CostEstimate(flops=20_000_000_000, transcendentals=0, bytes_accessed=0),
        name="tails",
    )(halo0, halo1)
    send, qeff, oeff = pl.pallas_call(
        local_kernel,
        out_shape=(
            jax.ShapeDtypeStruct((160, 128), BF16),
            jax.ShapeDtypeStruct((2, 128, 128), BF16),
            jax.ShapeDtypeStruct((2, 96, 128), F32),
        ),
        in_specs=[vmem] * 7,
        out_specs=(vmem, vmem, vmem),
        scratch_shapes=[
            pltpu.VMEM((half // 128, 128, 128), F32),
            pltpu.VMEM((256, width), BF16),
        ],
        compiler_params=params,
        name="local",
    )(own.reshape(n_head * 8, half), mate.reshape(n_head * 8, half), tails, weights, lr_rows, taps, base)

    groups = [[2 * j + (c + j) % 2 for j in range(n_seq // 2)] for c in range(2)]
    received = lax.all_gather(send, "seq", axis_index_groups=groups)
    rows = pl.pallas_call(
        chain_kernel,
        out_shape=jax.ShapeDtypeStruct((128, 128), F32),
        in_specs=[vmem] * 4,
        out_specs=vmem,
        compiler_params=params,
        name="chain",
    )(received, qeff, oeff, w_init)
    other = lax.ppermute(rows, "seq", swap)
    partial = pl.pallas_call(
        output_kernel,
        out_shape=jax.ShapeDtypeStruct((n_head * 8, half), BF16),
        in_specs=[vmem] * 3,
        out_specs=vmem,
        compiler_params=params,
        name="output",
    )(rows, other, w_out)
    parts = lax.all_to_all(partial.reshape(n_head, 8, half), "head", 0, 0)
    return pl.pallas_call(
        total_kernel,
        out_shape=jax.ShapeDtypeStruct(tokens.shape, BF16),
        in_specs=[vmem],
        out_specs=vmem,
        scratch_shapes=[pltpu.VMEM((half // 128, 8, 128), F32)],
        compiler_params=params,
        name="total",
    )(parts)


def solution(mesh):
    placed = (
        P(("seq", "head"), None),
        P(None, "head", None),
        P("head", None),
        P("head"),
        P(None, None, "head"),
        P(None, "head", None, None),
        P("head", None),
    )
    return jax.shard_map(
        shards, mesh=mesh, in_specs=placed, out_specs=P(("seq", "head"), None), check_vma=False
    )
```

```python
import jax
import jax.numpy as jnp
from jax import lax
from jax.experimental import pallas as pl
from jax.experimental.pallas import tpu as pltpu
from jax.sharding import PartitionSpec as P

MB = 16
KERNEL = 4
EPSILON = 1e-05
F32 = jnp.float32
BF16 = jnp.bfloat16


def mm(a, b, ca=1, cb=0):
    return lax.dot_general(a, b, (((ca,), (cb,)), ((), ())), preferred_element_type=F32)


def cat(parts, axis):
    return jnp.concatenate(parts, axis=axis)


def normed(u):
    centred = u - jnp.mean(u, axis=0, keepdims=True)
    return centred * lax.rsqrt(jnp.mean(centred * centred, axis=0, keepdims=True) + EPSILON)


def role_of(place):
    return (place + place // 2) % 2


def fold_kernel(tokens_ref, out_hbm, wide_ref, block_ref, sems):
    half = block_ref.shape[1]
    for j in range(half // 128):
        for part in range(2):
            piece = tokens_ref[:, part * half + j * 128:part * half + (j + 1) * 128].astype(F32)
            wide_ref[j, pl.ds(part, 4, stride=2), :] = piece
        block_ref[:, j * 128:(j + 1) * 128] = wide_ref[j].astype(BF16)
    copies = [pltpu.make_async_copy(block_ref, out_hbm.at[i], sems.at[i]) for i in range(out_hbm.shape[0])]
    for c in copies:
        c.start()
    for c in copies:
        c.wait()


def prepare_kernel(w_hbm, lrw_ref, conv_ref, base_ref, w_ref, lrp_ref, taps_ref, rate_ref, sem):
    role = role_of(lax.axis_index("seq"))
    used = pl.ds(pl.multiple_of(64 * role, 64), 128)
    fetch = pltpu.make_async_copy(w_hbm.at[:, used, :], w_ref, sem)
    fetch.start()
    lrw = lrw_ref[...].astype(F32)
    whole = jnp.where(role == 0, lrw[0:1], lrw[2:3])
    lrp_ref[...] = cat([whole, lrw[1:2], jnp.zeros((14, lrw.shape[1]), F32)], 0).astype(BF16)
    inner = conv_ref.shape[2]
    taps_rows = cat([conv_ref[0], conv_ref[1]], 0)
    taps_ref[...] = cat([taps_rows, jnp.zeros((2 * KERNEL, 256 - inner), F32)], 1).T
    base = base_ref[...] / MB
    rate_ref[...] = jnp.zeros_like(rate_ref)
    rate_ref[0:1, :] = jnp.broadcast_to(jnp.where(role == 0, base[0:1, 0:1], base[0:1, 2:3]), (1, 128))
    rate_ref[1:2, :] = jnp.broadcast_to(base[0:1, 1:2], (1, 128))
    fetch.wait()


def spread(src_ref, wide_ref, out_ref, row):
    half = src_ref.shape[1]
    for j in range(half // 128):
        wide_ref[j] = src_ref[:, j * 128:(j + 1) * 128].astype(F32)
        for part in range(2):
            cols = slice(part * half + j * 128, part * half + (j + 1) * 128)
            out_ref[pl.ds(row, 64), cols] = wide_ref[j, pl.ds(part, 64, stride=2), :].astype(BF16)


def tail_kernel(halo0_ref, halo1_ref, out_ref, wide_ref):
    core = lax.axis_index("seq") % 2
    half = halo0_ref.shape[1]
    halo = jnp.where(core == 0, halo0_ref[...].astype(F32), halo1_ref[...].astype(F32))
    for j in range(half // 128):
        wide_ref[j, 0:24, :] = jnp.zeros((24, 128), F32)
        wide_ref[j, 24:32, :] = halo[:, j * 128:(j + 1) * 128]
        for part in range(2):
            cols = slice(part * half + j * 128, part * half + (j + 1) * 128)
            out_ref[:, cols] = wide_ref[j, pl.ds(part, 16, stride=2), :].astype(BF16)


def local_kernel(own_ref, mate_ref, tail_ref, w_ref, lrp_ref, taps_ref, rate_ref,
                 send_ref, qeff_ref, oeff_ref, wide_ref, xall_ref):
    place = lax.axis_index("seq")
    core = place % 2
    role = role_of(place)
    spread(own_ref, wide_ref, xall_ref, pl.multiple_of(64 * core, 64))
    spread(mate_ref, wide_ref, xall_ref, pl.multiple_of(64 * (1 - core), 64))
    xall_ref[240:256, :] = tail_ref[...]
    at = pl.multiple_of(128 * role, 64)
    whole = pl.ds(pl.multiple_of(64 * role, 64), 64)
    shared = pl.ds(pl.multiple_of(64 * (1 - role), 64), 64)
    mid = pl.ds(pl.multiple_of(64 - 32 * role, 32), 32)
    rows = cat([
        w_ref[0, whole, :], w_ref[0, shared, :], w_ref[1, whole, :], w_ref[1, shared, :],
        w_ref[2, whole, :], w_ref[2, mid, :], lrp_ref[...],
    ], 0)
    proj = mm(rows, xall_ref[...], 1, 1)
    lane = lax.broadcasted_iota(jnp.int32, (128, 128), 1)
    taps = cat([taps_ref[pl.ds(at, 64), :], taps_ref[64:128, :]], 0)
    convs = []
    for i in range(2):
        raw = proj[128 * i:128 * i + 128, 0:128].astype(BF16).astype(F32)
        edge = proj[128 * i:128 * i + 128, 128:256].astype(BF16).astype(F32)
        first = KERNEL * i
        conv = taps[:, first + KERNEL - 1:first + KERNEL] * raw
        for back in range(1, KERNEL):
            moved = jnp.where(lane < back, pltpu.roll(edge, back, 1), pltpu.roll(raw, back, 1))
            conv = conv + taps[:, first + KERNEL - 1 - back:first + KERNEL - back] * moved
        convs.append(conv)

    src = lax.broadcasted_iota(jnp.int32, (128, 128), 0)
    dst = lax.broadcasted_iota(jnp.int32, (128, 128), 1)
    strict = dst // MB > src // MB
    eye = jnp.where(src == dst, 1.0, 0.0).astype(F32)

    two = range(2)
    q = [convs[0][64 * i:64 * i + 64] for i in two]
    k = [convs[1][64 * i:64 * i + 64] for i in two]
    k = [x * lax.rsqrt((jnp.mean(x * x, axis=0, keepdims=True) + EPSILON) * 64) for x in k]
    rate = [jax.nn.sigmoid(proj[352 + i:353 + i, 0:128]) * rate_ref[i:i + 1, :] for i in two]
    v = [proj[256:320, 0:128], proj[320:352, 0:128]]
    kb = [x.astype(BF16) for x in k]
    kt = [x.T for x in kb]
    grams = [mm(kt[i], cat([kb[i], q[i].astype(BF16)], 1)) for i in two]
    u = [jnp.where(strict, grams[i][:, 0:128], 0.0) * rate[i] for i in two]
    ub = [x.astype(BF16) for x in u]
    u2 = [mm(x, x) for x in ub]
    u2b = [x.astype(BF16) for x in u2]
    u4 = [mm(x, x).astype(BF16) for x in u2b]
    u3 = [mm(ub[i], u2b[i]) for i in two]
    t1 = [eye - u[i] + u2[i] - u3[i] for i in two]
    t = [t1[i] + mm(t1[i].astype(BF16), u4[i]) for i in two]
    rev = [t[i].T * rate[i] for i in two]
    ways = [[x.T.astype(BF16) for x in rev], [x.astype(BF16) for x in rev]]
    seen = [[jnp.where(mask, grams[i][:, 128:256], 0.0).astype(BF16) for i in two] for mask in (dst >= src, dst <= src)]
    solved = [[mm(ways[w][i], cat([seen[w][i], kt[i]], 1)).astype(BF16) for i in two] for w in two]
    stacked = [cat([kb[i], v[i].astype(BF16)], 0) for i in two]
    both = [[mm(stacked[i], solved[w][i]) for i in two] for w in two]
    for w in two:
        for i in two:
            qeff_ref[w, 64 * i:64 * i + 64, :] = (q[i] - both[w][i][0:64, 0:128]).astype(BF16)
            oeff_ref[w, 64 * i:64 * i + v[i].shape[0], :] = both[w][i][64:, 0:128]
    maps = [[(-both[w][i][0:64, 128:192], both[w][i][64:, 128:192]) for w in two] for i in two]
    (a0, b0), (a1, b1) = maps[0][0], maps[1][0]
    send_ref[0:64, :] = cat([a0, a1], 1).astype(BF16)
    for way in range(2):
        b0, b1 = maps[0][way][1], maps[1][way][1]
        packed = cat([b0[0:48], cat([b0[48:64], b1], 0)], 1)
        send_ref[64 + 48 * way:112 + 48 * way, :] = packed.astype(BF16)


def chain_kernel(maps_ref, qeff_ref, oeff_ref, init_ref, out_ref):
    place = lax.axis_index("seq")
    role = role_of(place)
    chip = place // 2
    chips = maps_ref.shape[0]
    states = []
    for way in range(2):
        shared = init_ref[way, 1, pl.ds(pl.multiple_of(32 * role, 32), 32), :]
        states.append([init_ref[way, 2 * role], shared])
    for i in range(chips - 1):
        for way in range(2):
            j = i if way == 0 else chips - 1 - i
            live = (j < chip) if way == 0 else (j > chip)
            block = jnp.where(live, maps_ref[j].astype(F32), 0.0)
            whole, shared = states[way]
            at = 64 + 48 * way
            steps = block[0:64].astype(BF16)
            b0 = cat([block[at:at + 48, 0:64], block[at:at + 16, 64:128]], 0)
            b1 = block[at + 16:at + 48, 64:128]
            new0 = (whole + b0) + mm(whole.astype(BF16), steps[:, 0:64], 1, way)
            new1 = (shared + b1) + mm(shared.astype(BF16), steps[:, 64:128], 1, way)
            states[way] = [new0, new1]
    sums = None
    for way in range(2):
        whole = mm(states[way][0].astype(BF16), qeff_ref[way, 0:64, :]) + oeff_ref[way, 0:64, :]
        sums = normed(whole) if sums is None else sums + normed(whole)
        shared = mm(states[way][1].astype(BF16), qeff_ref[way, 64:128, :]) + oeff_ref[way, 64:96, :]
        out_ref[64 + 32 * way:96 + 32 * way, :] = shared
    out_ref[0:64, :] = sums


def output_kernel(mine_ref, mate_ref, w_ref, out_ref):
    place = lax.axis_index("seq")
    core = place % 2
    role = role_of(place)
    mine = mine_ref[...]
    mate = mate_ref[...]
    low = jnp.where(role == 0, mine, mate)
    high = jnp.where(role == 0, mate, mine)
    middle = normed(cat([low[64:96], high[64:96]], 0)) + normed(cat([low[96:128], high[96:128]], 0))
    hidden = cat([low[0:64], middle, high[0:64]], 0).astype(BF16)
    row = lax.broadcasted_iota(jnp.int32, (128, 128), 0)
    col = lax.broadcasted_iota(jnp.int32, (128, 128), 1)
    pick = jnp.where(col == row // 2 + 64 * core, 1.0, 0.0).astype(BF16)
    twice = mm(pick, hidden, 1, 1).astype(BF16)
    half = out_ref.shape[1]
    even = lax.broadcasted_iota(jnp.int32, (128, half), 0) % 2 == 0
    first = mm(twice, w_ref[:, 0:half])
    second = mm(twice, w_ref[:, half:2 * half])
    out_ref[...] = jnp.where(even, first, second).astype(BF16)


def total_kernel(parts_ref, out_ref, wide_ref):
    acc = parts_ref[0].astype(F32)
    for i in range(1, parts_ref.shape[0]):
        acc = acc + parts_ref[i].astype(F32)
    half = acc.shape[1]
    for j in range(half // 128):
        wide_ref[j] = acc[:, j * 128:(j + 1) * 128]
        for part in range(2):
            out_ref[:, part * half + j * 128:part * half + (j + 1) * 128] = (
                wide_ref[j, pl.ds(part, 4, stride=2), :].astype(BF16))


def shards(tokens, w_qkv, lr_weight, lr_base, conv_weight, w_init, w_out):
    width = tokens.shape[1]
    half = width // 2
    inner = w_qkv.shape[1]
    n_seq = lax.axis_size("seq")
    n_head = lax.axis_size("head")
    params = pltpu.CompilerParams(vmem_limit_bytes=24 * 1024 * 1024)
    vmem = pl.BlockSpec(memory_space=pltpu.VMEM)
    hbm = pl.BlockSpec(memory_space=pl.ANY)

    folded = pl.pallas_call(
        fold_kernel,
        out_shape=jax.ShapeDtypeStruct((n_head, 8, half), BF16),
        in_specs=[vmem],
        out_specs=hbm,
        scratch_shapes=[
            pltpu.VMEM((half // 128, 8, 128), F32),
            pltpu.VMEM((8, half), BF16),
            pltpu.SemaphoreType.DMA((n_head,)),
        ],
        compiler_params=params,
        name="fold",
    )(tokens)
    own = lax.all_to_all(folded, "head", 0, 0)
    weights, lr_rows, taps, base = pl.pallas_call(
        prepare_kernel,
        out_shape=(
            jax.ShapeDtypeStruct((3, 128, width), BF16),
            jax.ShapeDtypeStruct((16, width), BF16),
            jax.ShapeDtypeStruct((256, 2 * KERNEL), F32),
            jax.ShapeDtypeStruct((8, 128), F32),
        ),
        in_specs=[hbm] + [vmem] * 3,
        out_specs=(vmem,) * 4,
        scratch_shapes=[pltpu.SemaphoreType.DMA(())],
        compiler_params=params,
        name="prepare",
    )(w_qkv, lr_weight, conv_weight, lr_base.reshape(1, lr_base.shape[0]))
    own, weights = lax.optimization_barrier((own, weights))
    swap = [(i, i ^ 1) for i in range(n_seq)]
    mate = lax.ppermute(own, "seq", swap)
    tail = own[n_head - 1]
    halo0 = lax.ppermute(tail, "seq", [(i, i + 1) for i in range(1, n_seq - 1, 2)])
    halo1 = lax.ppermute(tail, "seq", [(i, i + 2) for i in range(1, n_seq - 2, 2)])
    tails = pl.pallas_call(
        tail_kernel,
        out_shape=jax.ShapeDtypeStruct((16, width), BF16),
        in_specs=[vmem] * 2,
        out_specs=vmem,
        scratch_shapes=[pltpu.VMEM((half // 128, 32, 128), F32)],
        compiler_params=params,
        cost_estimate=pl.CostEstimate(flops=20_000_000_000, transcendentals=0, bytes_accessed=0),
        name="tails",
    )(halo0, halo1)
    send, qeff, oeff = pl.pallas_call(
        local_kernel,
        out_shape=(
            jax.ShapeDtypeStruct((160, 128), BF16),
            jax.ShapeDtypeStruct((2, 128, 128), BF16),
            jax.ShapeDtypeStruct((2, 96, 128), F32),
        ),
        in_specs=[vmem] * 7,
        out_specs=(vmem, vmem, vmem),
        scratch_shapes=[
            pltpu.VMEM((half // 128, 128, 128), F32),
            pltpu.VMEM((256, width), BF16),
        ],
        compiler_params=params,
        name="local",
    )(own.reshape(n_head * 8, half), mate.reshape(n_head * 8, half), tails, weights, lr_rows, taps, base)

    groups = [[2 * j + (c + j) % 2 for j in range(n_seq // 2)] for c in range(2)]
    received = lax.all_gather(send, "seq", axis_index_groups=groups)
    rows = pl.pallas_call(
        chain_kernel,
        out_shape=jax.ShapeDtypeStruct((128, 128), F32),
        in_specs=[vmem] * 4,
        out_specs=vmem,
        compiler_params=params,
        name="chain",
    )(received, qeff, oeff, w_init)
    other = lax.ppermute(rows, "seq", swap)
    partial = pl.pallas_call(
        output_kernel,
        out_shape=jax.ShapeDtypeStruct((n_head * 8, half), BF16),
        in_specs=[vmem] * 3,
        out_specs=vmem,
        compiler_params=params,
        name="output",
    )(rows, other, w_out)
    parts = lax.all_to_all(partial.reshape(n_head, 8, half), "head", 0, 0)
    return pl.pallas_call(
        total_kernel,
        out_shape=jax.ShapeDtypeStruct(tokens.shape, BF16),
        in_specs=[vmem],
        out_specs=vmem,
        scratch_shapes=[pltpu.VMEM((half // 128, 8, 128), F32)],
        compiler_params=params,
        name="total",
    )(parts)


def solution(mesh):
    placed = (
        P(("seq", "head"), None),
        P(None, "head", None),
        P("head", None),
        P("head"),
        P(None, None, "head"),
        P(None, "head", None, None),
        P("head", None),
    )
    return jax.shard_map(
        shards, mesh=mesh, in_specs=placed, out_specs=P(("seq", "head"), None), check_vma=False
    )
```

```python
import jax
import jax.numpy as jnp
from jax import lax
from jax.experimental import pallas as pl
from jax.experimental.pallas import tpu as pltpu
from jax.sharding import PartitionSpec as P

MB = 16
KERNEL = 4
EPSILON = 1e-05
F32 = jnp.float32
BF16 = jnp.bfloat16


def mm(a, b, ca=1, cb=0):
    return lax.dot_general(a, b, (((ca,), (cb,)), ((), ())), preferred_element_type=F32)


def cat(parts, axis):
    return jnp.concatenate(parts, axis=axis)


def normed(u):
    centred = u - jnp.mean(u, axis=0, keepdims=True)
    return centred * lax.rsqrt(jnp.mean(centred * centred, axis=0, keepdims=True) + EPSILON)


def role_of(place):
    return (place + place // 2) % 2


def fold_kernel(tokens_ref, out_hbm, wide_ref, block_ref, sems):
    half = block_ref.shape[1]
    for j in range(half // 128):
        for part in range(2):
            piece = tokens_ref[:, part * half + j * 128:part * half + (j + 1) * 128].astype(F32)
            wide_ref[j, pl.ds(part, 4, stride=2), :] = piece
        block_ref[:, j * 128:(j + 1) * 128] = wide_ref[j].astype(BF16)
    copies = [pltpu.make_async_copy(block_ref, out_hbm.at[i], sems.at[i]) for i in range(out_hbm.shape[0])]
    for c in copies:
        c.start()
    for c in copies:
        c.wait()


def prepare_kernel(w_hbm, lrw_ref, conv_ref, base_ref, w_ref, lrp_ref, taps_ref, rate_ref, sem):
    role = role_of(lax.axis_index("seq"))
    used = pl.ds(pl.multiple_of(64 * role, 64), 128)
    fetch = pltpu.make_async_copy(w_hbm.at[:, used, :], w_ref, sem)
    fetch.start()
    lrw = lrw_ref[...].astype(F32)
    whole = jnp.where(role == 0, lrw[0:1], lrw[2:3])
    lrp_ref[...] = cat([whole, lrw[1:2], jnp.zeros((14, lrw.shape[1]), F32)], 0).astype(BF16)
    inner = conv_ref.shape[2]
    taps_rows = cat([conv_ref[0], conv_ref[1]], 0)
    taps_ref[...] = cat([taps_rows, jnp.zeros((2 * KERNEL, 256 - inner), F32)], 1).T
    base = base_ref[...] / MB
    rate_ref[...] = jnp.zeros_like(rate_ref)
    rate_ref[0:1, :] = jnp.broadcast_to(jnp.where(role == 0, base[0:1, 0:1], base[0:1, 2:3]), (1, 128))
    rate_ref[1:2, :] = jnp.broadcast_to(base[0:1, 1:2], (1, 128))
    fetch.wait()


def spread(src_ref, wide_ref, out_ref, row):
    half = src_ref.shape[1]
    for j in range(half // 128):
        wide_ref[j] = src_ref[:, j * 128:(j + 1) * 128].astype(F32)
        for part in range(2):
            cols = slice(part * half + j * 128, part * half + (j + 1) * 128)
            out_ref[pl.ds(row, 64), cols] = wide_ref[j, pl.ds(part, 64, stride=2), :].astype(BF16)


def tail_kernel(halo0_ref, halo1_ref, out_ref, wide_ref):
    core = lax.axis_index("seq") % 2
    half = halo0_ref.shape[1]
    halo = jnp.where(core == 0, halo0_ref[...].astype(F32), halo1_ref[...].astype(F32))
    for j in range(half // 128):
        wide_ref[j, 0:24, :] = jnp.zeros((24, 128), F32)
        wide_ref[j, 24:32, :] = halo[:, j * 128:(j + 1) * 128]
        for part in range(2):
            cols = slice(part * half + j * 128, part * half + (j + 1) * 128)
            out_ref[:, cols] = wide_ref[j, pl.ds(part, 16, stride=2), :].astype(BF16)


def local_kernel(own_ref, mate_ref, tail_ref, w_ref, lrp_ref, taps_ref, rate_ref,
                 send_ref, qeff_ref, oeff_ref, wide_ref, xall_ref):
    place = lax.axis_index("seq")
    core = place % 2
    role = role_of(place)
    spread(own_ref, wide_ref, xall_ref, pl.multiple_of(64 * core, 64))
    spread(mate_ref, wide_ref, xall_ref, pl.multiple_of(64 * (1 - core), 64))
    xall_ref[240:256, :] = tail_ref[...]
    at = pl.multiple_of(128 * role, 64)
    whole = pl.ds(pl.multiple_of(64 * role, 64), 64)
    shared = pl.ds(pl.multiple_of(64 * (1 - role), 64), 64)
    mid = pl.ds(pl.multiple_of(64 - 32 * role, 32), 32)
    rows = cat([
        w_ref[0, whole, :], w_ref[0, shared, :], w_ref[1, whole, :], w_ref[1, shared, :],
        w_ref[2, whole, :], w_ref[2, mid, :], lrp_ref[...],
    ], 0)
    proj = mm(rows, xall_ref[...], 1, 1)
    lane = lax.broadcasted_iota(jnp.int32, (128, 128), 1)
    taps = cat([taps_ref[pl.ds(at, 64), :], taps_ref[64:128, :]], 0)
    convs = []
    for i in range(2):
        raw = proj[128 * i:128 * i + 128, 0:128].astype(BF16).astype(F32)
        edge = proj[128 * i:128 * i + 128, 128:256].astype(BF16).astype(F32)
        first = KERNEL * i
        conv = taps[:, first + KERNEL - 1:first + KERNEL] * raw
        for back in range(1, KERNEL):
            moved = jnp.where(lane < back, pltpu.roll(edge, back, 1), pltpu.roll(raw, back, 1))
            conv = conv + taps[:, first + KERNEL - 1 - back:first + KERNEL - back] * moved
        convs.append(conv)

    src = lax.broadcasted_iota(jnp.int32, (128, 128), 0)
    dst = lax.broadcasted_iota(jnp.int32, (128, 128), 1)
    strict = dst // MB > src // MB
    eye = jnp.where(src == dst, 1.0, 0.0).astype(F32)

    two = range(2)
    q = [convs[0][64 * i:64 * i + 64] for i in two]
    k = [convs[1][64 * i:64 * i + 64] for i in two]
    k = [x * lax.rsqrt((jnp.mean(x * x, axis=0, keepdims=True) + EPSILON) * 64) for x in k]
    rate = [jax.nn.sigmoid(proj[352 + i:353 + i, 0:128]) * rate_ref[i:i + 1, :] for i in two]
    v = [proj[256:320, 0:128], proj[320:352, 0:128]]
    kb = [x.astype(BF16) for x in k]
    kt = [x.T for x in kb]
    grams = [mm(kt[i], cat([kb[i], q[i].astype(BF16)], 1)) for i in two]
    u = [jnp.where(strict, grams[i][:, 0:128], 0.0) * rate[i] for i in two]
    ub = [x.astype(BF16) for x in u]
    u2 = [mm(x, x) for x in ub]
    u2b = [x.astype(BF16) for x in u2]
    u4 = [mm(x, x).astype(BF16) for x in u2b]
    u3 = [mm(ub[i], u2b[i]) for i in two]
    t1 = [eye - u[i] + u2[i] - u3[i] for i in two]
    t = [t1[i] + mm(t1[i].astype(BF16), u4[i]) for i in two]
    rev = [t[i].T * rate[i] for i in two]
    ways = [[x.T.astype(BF16) for x in rev], [x.astype(BF16) for x in rev]]
    seen = [[jnp.where(mask, grams[i][:, 128:256], 0.0).astype(BF16) for i in two] for mask in (dst >= src, dst <= src)]
    solved = [[mm(ways[w][i], cat([seen[w][i], kt[i]], 1)).astype(BF16) for i in two] for w in two]
    stacked = [cat([kb[i], v[i].astype(BF16)], 0) for i in two]
    both = [[mm(stacked[i], solved[w][i]) for i in two] for w in two]
    for w in two:
        for i in two:
            qeff_ref[w, 64 * i:64 * i + 64, :] = (q[i] - both[w][i][0:64, 0:128]).astype(BF16)
            oeff_ref[w, 64 * i:64 * i + v[i].shape[0], :] = both[w][i][64:, 0:128]
    maps = [[(-both[w][i][0:64, 128:192], both[w][i][64:, 128:192]) for w in two] for i in two]
    (a0, b0), (a1, b1) = maps[0][0], maps[1][0]
    send_ref[0:64, :] = cat([a0, a1], 1).astype(BF16)
    for way in range(2):
        b0, b1 = maps[0][way][1], maps[1][way][1]
        packed = cat([b0[0:48], cat([b0[48:64], b1], 0)], 1)
        send_ref[64 + 48 * way:112 + 48 * way, :] = packed.astype(BF16)


def chain_kernel(maps_ref, qeff_ref, oeff_ref, init_ref, out_ref):
    place = lax.axis_index("seq")
    role = role_of(place)
    chip = place // 2
    chips = maps_ref.shape[0]
    states = []
    for way in range(2):
        shared = init_ref[way, 1, pl.ds(pl.multiple_of(32 * role, 32), 32), :]
        states.append([init_ref[way, 2 * role], shared])
    def fetched(i, way):
        j = i if way == 0 else chips - 1 - i
        live = (j < chip) if way == 0 else (j > chip)
        block = jnp.where(live, maps_ref[j].astype(F32), 0.0)
        at = 64 + 48 * way
        b0 = cat([block[at:at + 48, 0:64], block[at:at + 16, 64:128]], 0)
        return [(block[0:64, 0:64], b0), (block[0:64, 64:128], block[at + 16:at + 48, 64:128])]

    first = chips // 2
    later = [None, None]
    for i in range(first):
        for way in range(2):
            near = fetched(i, way)
            states[way] = [
                (w + off) + mm(w.astype(BF16), step.astype(BF16), 1, way) for w, (step, off) in zip(states[way], near)
            ]
            if first + i < chips - 1:
                far = fetched(first + i, way)
                fresh = [cat([step if way == 0 else step.T, off], 0) for step, off in far]
                if later[way] is None:
                    later[way] = fresh
                else:
                    later[way] = [
                        (x + f) + mm(x.astype(BF16), step.astype(BF16), 1, way) for x, f, (step, off) in zip(later[way], fresh, far)
                    ]
    for way in range(2):
        states[way] = [
            (w + x[64:]) + mm(w.astype(BF16), x[0:64].astype(BF16)) for w, x in zip(states[way], later[way])
        ]
    sums = None
    for way in range(2):
        whole = mm(states[way][0].astype(BF16), qeff_ref[way, 0:64, :]) + oeff_ref[way, 0:64, :]
        sums = normed(whole) if sums is None else sums + normed(whole)
        shared = mm(states[way][1].astype(BF16), qeff_ref[way, 64:128, :]) + oeff_ref[way, 64:96, :]
        out_ref[64 + 32 * way:96 + 32 * way, :] = shared
    out_ref[0:64, :] = sums


def output_kernel(mine_ref, mate_ref, w_ref, out_ref):
    place = lax.axis_index("seq")
    core = place % 2
    role = role_of(place)
    mine = mine_ref[...]
    mate = mate_ref[...]
    low = jnp.where(role == 0, mine, mate)
    high = jnp.where(role == 0, mate, mine)
    middle = normed(cat([low[64:96], high[64:96]], 0)) + normed(cat([low[96:128], high[96:128]], 0))
    hidden = cat([low[0:64], middle, high[0:64]], 0).astype(BF16)
    row = lax.broadcasted_iota(jnp.int32, (128, 128), 0)
    col = lax.broadcasted_iota(jnp.int32, (128, 128), 1)
    pick = jnp.where(col == row // 2 + 64 * core, 1.0, 0.0).astype(BF16)
    twice = mm(pick, hidden, 1, 1).astype(BF16)
    half = out_ref.shape[1]
    even = lax.broadcasted_iota(jnp.int32, (128, half), 0) % 2 == 0
    first = mm(twice, w_ref[:, 0:half])
    second = mm(twice, w_ref[:, half:2 * half])
    out_ref[...] = jnp.where(even, first, second).astype(BF16)


def total_kernel(parts_ref, out_ref, wide_ref):
    acc = parts_ref[0].astype(F32)
    for i in range(1, parts_ref.shape[0]):
        acc = acc + parts_ref[i].astype(F32)
    half = acc.shape[1]
    for j in range(half // 128):
        wide_ref[j] = acc[:, j * 128:(j + 1) * 128]
        for part in range(2):
            out_ref[:, part * half + j * 128:part * half + (j + 1) * 128] = (
                wide_ref[j, pl.ds(part, 4, stride=2), :].astype(BF16))


def shards(tokens, w_qkv, lr_weight, lr_base, conv_weight, w_init, w_out):
    width = tokens.shape[1]
    half = width // 2
    inner = w_qkv.shape[1]
    n_seq = lax.axis_size("seq")
    n_head = lax.axis_size("head")
    params = pltpu.CompilerParams(vmem_limit_bytes=24 * 1024 * 1024)
    vmem = pl.BlockSpec(memory_space=pltpu.VMEM)
    hbm = pl.BlockSpec(memory_space=pl.ANY)

    folded = pl.pallas_call(
        fold_kernel,
        out_shape=jax.ShapeDtypeStruct((n_head, 8, half), BF16),
        in_specs=[vmem],
        out_specs=hbm,
        scratch_shapes=[
            pltpu.VMEM((half // 128, 8, 128), F32),
            pltpu.VMEM((8, half), BF16),
            pltpu.SemaphoreType.DMA((n_head,)),
        ],
        compiler_params=params,
        name="fold",
    )(tokens)
    own = lax.all_to_all(folded, "head", 0, 0)
    weights, lr_rows, taps, base = pl.pallas_call(
        prepare_kernel,
        out_shape=(
            jax.ShapeDtypeStruct((3, 128, width), BF16),
            jax.ShapeDtypeStruct((16, width), BF16),
            jax.ShapeDtypeStruct((256, 2 * KERNEL), F32),
            jax.ShapeDtypeStruct((8, 128), F32),
        ),
        in_specs=[hbm] + [vmem] * 3,
        out_specs=(vmem,) * 4,
        scratch_shapes=[pltpu.SemaphoreType.DMA(())],
        compiler_params=params,
        name="prepare",
    )(w_qkv, lr_weight, conv_weight, lr_base.reshape(1, lr_base.shape[0]))
    own, weights = lax.optimization_barrier((own, weights))
    swap = [(i, i ^ 1) for i in range(n_seq)]
    mate = lax.ppermute(own, "seq", swap)
    tail = own[n_head - 1]
    halo0 = lax.ppermute(tail, "seq", [(i, i + 1) for i in range(1, n_seq - 1, 2)])
    halo1 = lax.ppermute(tail, "seq", [(i, i + 2) for i in range(1, n_seq - 2, 2)])
    tails = pl.pallas_call(
        tail_kernel,
        out_shape=jax.ShapeDtypeStruct((16, width), BF16),
        in_specs=[vmem] * 2,
        out_specs=vmem,
        scratch_shapes=[pltpu.VMEM((half // 128, 32, 128), F32)],
        compiler_params=params,
        cost_estimate=pl.CostEstimate(flops=20_000_000_000, transcendentals=0, bytes_accessed=0),
        name="tails",
    )(halo0, halo1)
    send, qeff, oeff = pl.pallas_call(
        local_kernel,
        out_shape=(
            jax.ShapeDtypeStruct((160, 128), BF16),
            jax.ShapeDtypeStruct((2, 128, 128), BF16),
            jax.ShapeDtypeStruct((2, 96, 128), F32),
        ),
        in_specs=[vmem] * 7,
        out_specs=(vmem, vmem, vmem),
        scratch_shapes=[
            pltpu.VMEM((half // 128, 128, 128), F32),
            pltpu.VMEM((256, width), BF16),
        ],
        compiler_params=params,
        name="local",
    )(own.reshape(n_head * 8, half), mate.reshape(n_head * 8, half), tails, weights, lr_rows, taps, base)

    groups = [[2 * j + (c + j) % 2 for j in range(n_seq // 2)] for c in range(2)]
    received = lax.all_gather(send, "seq", axis_index_groups=groups)
    rows = pl.pallas_call(
        chain_kernel,
        out_shape=jax.ShapeDtypeStruct((128, 128), F32),
        in_specs=[vmem] * 4,
        out_specs=vmem,
        compiler_params=params,
        name="chain",
    )(received, qeff, oeff, w_init)
    other = lax.ppermute(rows, "seq", swap)
    partial = pl.pallas_call(
        output_kernel,
        out_shape=jax.ShapeDtypeStruct((n_head * 8, half), BF16),
        in_specs=[vmem] * 3,
        out_specs=vmem,
        compiler_params=params,
        name="output",
    )(rows, other, w_out)
    parts = lax.all_to_all(partial.reshape(n_head, 8, half), "head", 0, 0)
    return pl.pallas_call(
        total_kernel,
        out_shape=jax.ShapeDtypeStruct(tokens.shape, BF16),
        in_specs=[vmem],
        out_specs=vmem,
        scratch_shapes=[pltpu.VMEM((half // 128, 8, 128), F32)],
        compiler_params=params,
        name="total",
    )(parts)


def solution(mesh):
    placed = (
        P(("seq", "head"), None),
        P(None, "head", None),
        P("head", None),
        P("head"),
        P(None, None, "head"),
        P(None, "head", None, None),
        P("head", None),
    )
    return jax.shard_map(
        shards, mesh=mesh, in_specs=placed, out_specs=P(("seq", "head"), None), check_vma=False
    )
```

```python
import jax
import jax.numpy as jnp
from jax import lax
from jax.experimental import pallas as pl
from jax.experimental.pallas import tpu as pltpu
from jax.sharding import PartitionSpec as P

MB = 16
KERNEL = 4
EPSILON = 1e-05
F32 = jnp.float32
BF16 = jnp.bfloat16


def mm(a, b, ca=1, cb=0):
    return lax.dot_general(a, b, (((ca,), (cb,)), ((), ())), preferred_element_type=F32)


def cat(parts, axis):
    return jnp.concatenate(parts, axis=axis)


def normed(u):
    centred = u - jnp.mean(u, axis=0, keepdims=True)
    return centred * lax.rsqrt(jnp.mean(centred * centred, axis=0, keepdims=True) + EPSILON)


def role_of(place):
    return (place + place // 2) % 2


def fold_kernel(tokens_ref, out_hbm, wide_ref, block_ref, sems):
    half = block_ref.shape[1]
    for j in range(half // 128):
        for part in range(2):
            piece = tokens_ref[:, part * half + j * 128:part * half + (j + 1) * 128].astype(F32)
            wide_ref[j, pl.ds(part, 4, stride=2), :] = piece
        block_ref[:, j * 128:(j + 1) * 128] = wide_ref[j].astype(BF16)
    copies = [pltpu.make_async_copy(block_ref, out_hbm.at[i], sems.at[i]) for i in range(out_hbm.shape[0])]
    for c in copies:
        c.start()
    for c in copies:
        c.wait()


def prepare_kernel(w_hbm, lrw_ref, conv_ref, base_ref, w_ref, lrp_ref, taps_ref, rate_ref, sem):
    role = role_of(lax.axis_index("seq"))
    used = pl.ds(pl.multiple_of(64 * role, 64), 128)
    fetch = pltpu.make_async_copy(w_hbm.at[:, used, :], w_ref, sem)
    fetch.start()
    lrw = lrw_ref[...].astype(F32)
    whole = jnp.where(role == 0, lrw[0:1], lrw[2:3])
    lrp_ref[...] = cat([whole, lrw[1:2], jnp.zeros((14, lrw.shape[1]), F32)], 0).astype(BF16)
    inner = conv_ref.shape[2]
    taps_rows = cat([conv_ref[0], conv_ref[1]], 0)
    taps_ref[...] = cat([taps_rows, jnp.zeros((2 * KERNEL, 256 - inner), F32)], 1).T
    base = base_ref[...] / MB
    rate_ref[...] = jnp.zeros_like(rate_ref)
    rate_ref[0:1, :] = jnp.broadcast_to(jnp.where(role == 0, base[0:1, 0:1], base[0:1, 2:3]), (1, 128))
    rate_ref[1:2, :] = jnp.broadcast_to(base[0:1, 1:2], (1, 128))
    fetch.wait()


def spread(src_ref, wide_ref, out_ref, row):
    half = src_ref.shape[1]
    for j in range(half // 128):
        wide_ref[j] = src_ref[:, j * 128:(j + 1) * 128].astype(F32)
        for part in range(2):
            cols = slice(part * half + j * 128, part * half + (j + 1) * 128)
            out_ref[pl.ds(row, 64), cols] = wide_ref[j, pl.ds(part, 64, stride=2), :].astype(BF16)


def tail_kernel(halo0_ref, halo1_ref, out_ref, wide_ref):
    core = lax.axis_index("seq") % 2
    half = halo0_ref.shape[1]
    halo = jnp.where(core == 0, halo0_ref[...].astype(F32), halo1_ref[...].astype(F32))
    for j in range(half // 128):
        wide_ref[j, 0:24, :] = jnp.zeros((24, 128), F32)
        wide_ref[j, 24:32, :] = halo[:, j * 128:(j + 1) * 128]
        for part in range(2):
            cols = slice(part * half + j * 128, part * half + (j + 1) * 128)
            out_ref[:, cols] = wide_ref[j, pl.ds(part, 16, stride=2), :].astype(BF16)


def local_kernel(own_ref, mate_ref, tail_ref, w_ref, lrp_ref, taps_ref, rate_ref,
                 send_ref, qeff_ref, oeff_ref, wide_ref, xall_ref):
    place = lax.axis_index("seq")
    core = place % 2
    role = role_of(place)
    spread(own_ref, wide_ref, xall_ref, pl.multiple_of(64 * core, 64))
    spread(mate_ref, wide_ref, xall_ref, pl.multiple_of(64 * (1 - core), 64))
    xall_ref[240:256, :] = tail_ref[...]
    at = pl.multiple_of(128 * role, 64)
    whole = pl.ds(pl.multiple_of(64 * role, 64), 64)
    shared = pl.ds(pl.multiple_of(64 * (1 - role), 64), 64)
    mid = pl.ds(pl.multiple_of(64 - 32 * role, 32), 32)
    rows = cat([
        w_ref[0, whole, :], w_ref[0, shared, :], w_ref[1, whole, :], w_ref[1, shared, :],
        w_ref[2, whole, :], w_ref[2, mid, :], lrp_ref[...],
    ], 0)
    proj = mm(rows, xall_ref[...], 1, 1)
    lane = lax.broadcasted_iota(jnp.int32, (128, 128), 1)
    taps = cat([taps_ref[pl.ds(at, 64), :], taps_ref[64:128, :]], 0)
    convs = []
    for i in range(2):
        raw = proj[128 * i:128 * i + 128, 0:128].astype(BF16).astype(F32)
        edge = proj[128 * i:128 * i + 128, 128:256].astype(BF16).astype(F32)
        first = KERNEL * i
        conv = taps[:, first + KERNEL - 1:first + KERNEL] * raw
        for back in range(1, KERNEL):
            moved = jnp.where(lane < back, pltpu.roll(edge, back, 1), pltpu.roll(raw, back, 1))
            conv = conv + taps[:, first + KERNEL - 1 - back:first + KERNEL - back] * moved
        convs.append(conv)

    src = lax.broadcasted_iota(jnp.int32, (128, 128), 0)
    dst = lax.broadcasted_iota(jnp.int32, (128, 128), 1)
    strict = dst // MB > src // MB
    eye = jnp.where(src == dst, 1.0, 0.0).astype(F32)

    two = range(2)
    q = [convs[0][64 * i:64 * i + 64] for i in two]
    k = [convs[1][64 * i:64 * i + 64] for i in two]
    k = [x * lax.rsqrt((jnp.mean(x * x, axis=0, keepdims=True) + EPSILON) * 64) for x in k]
    rate = [jax.nn.sigmoid(proj[352 + i:353 + i, 0:128]) * rate_ref[i:i + 1, :] for i in two]
    v = [proj[256:320, 0:128], proj[320:352, 0:128]]
    kb = [x.astype(BF16) for x in k]
    kt = [x.T for x in kb]
    grams = [mm(kt[i], cat([kb[i], q[i].astype(BF16)], 1)) for i in two]
    u = [jnp.where(strict, grams[i][:, 0:128], 0.0) * rate[i] for i in two]
    ub = [x.astype(BF16) for x in u]
    u2 = [mm(x, x) for x in ub]
    u2b = [x.astype(BF16) for x in u2]
    u4 = [mm(x, x).astype(BF16) for x in u2b]
    u3 = [mm(ub[i], u2b[i]) for i in two]
    t1 = [eye - u[i] + u2[i] - u3[i] for i in two]
    t = [t1[i] + mm(t1[i].astype(BF16), u4[i]) for i in two]
    rev = [t[i].T * rate[i] for i in two]
    revb = [x.astype(BF16) for x in rev]
    seen = [[jnp.where(mask, grams[i][:, 128:256], 0.0).astype(BF16) for i in two] for mask in (dst >= src, dst <= src)]
    solved = [[mm(revb[i], cat([seen[w][i], kt[i]], 1), w, 0).astype(BF16) for i in two] for w in two]
    stacked = [cat([kb[i], v[i].astype(BF16)], 0) for i in two]
    both = [[mm(stacked[i], solved[w][i]) for i in two] for w in two]
    for w in two:
        for i in two:
            qeff_ref[w, 64 * i:64 * i + 64, :] = (q[i] - both[w][i][0:64, 0:128]).astype(BF16)
            oeff_ref[w, 64 * i:64 * i + v[i].shape[0], :] = both[w][i][64:, 0:128]
    maps = [[(-both[w][i][0:64, 128:192], both[w][i][64:, 128:192]) for w in two] for i in two]
    (a0, b0), (a1, b1) = maps[0][0], maps[1][0]
    send_ref[0:64, :] = cat([a0, a1], 1).astype(BF16)
    for way in range(2):
        b0, b1 = maps[0][way][1], maps[1][way][1]
        packed = cat([b0[0:48], cat([b0[48:64], b1], 0)], 1)
        send_ref[64 + 48 * way:112 + 48 * way, :] = packed.astype(BF16)


def chain_kernel(maps_ref, qeff_ref, oeff_ref, init_ref, out_ref):
    place = lax.axis_index("seq")
    role = role_of(place)
    chip = place // 2
    chips = maps_ref.shape[0]
    states = []
    for way in range(2):
        shared = init_ref[way, 1, pl.ds(pl.multiple_of(32 * role, 32), 32), :]
        states.append([init_ref[way, 2 * role], shared])
    for i in range(chips - 1):
        for way in range(2):
            j = i if way == 0 else chips - 1 - i
            live = (j < chip) if way == 0 else (j > chip)
            block = jnp.where(live, maps_ref[j].astype(F32), 0.0)
            whole, shared = states[way]
            at = 64 + 48 * way
            steps = block[0:64].astype(BF16)
            b0 = cat([block[at:at + 48, 0:64], block[at:at + 16, 64:128]], 0)
            b1 = block[at + 16:at + 48, 64:128]
            new0 = (whole + b0) + mm(whole.astype(BF16), steps[:, 0:64], 1, way)
            new1 = (shared + b1) + mm(shared.astype(BF16), steps[:, 64:128], 1, way)
            states[way] = [new0, new1]
    sums = None
    for way in range(2):
        whole = mm(states[way][0].astype(BF16), qeff_ref[way, 0:64, :]) + oeff_ref[way, 0:64, :]
        sums = normed(whole) if sums is None else sums + normed(whole)
        shared = mm(states[way][1].astype(BF16), qeff_ref[way, 64:128, :]) + oeff_ref[way, 64:96, :]
        out_ref[64 + 32 * way:96 + 32 * way, :] = shared
    out_ref[0:64, :] = sums


def output_kernel(mine_ref, mate_ref, w_ref, out_ref):
    place = lax.axis_index("seq")
    core = place % 2
    role = role_of(place)
    mine = mine_ref[...]
    mate = mate_ref[...]
    low = jnp.where(role == 0, mine, mate)
    high = jnp.where(role == 0, mate, mine)
    middle = normed(cat([low[64:96], high[64:96]], 0)) + normed(cat([low[96:128], high[96:128]], 0))
    hidden = cat([low[0:64], middle, high[0:64]], 0).astype(BF16)
    row = lax.broadcasted_iota(jnp.int32, (128, 128), 0)
    col = lax.broadcasted_iota(jnp.int32, (128, 128), 1)
    pick = jnp.where(col == row // 2 + 64 * core, 1.0, 0.0).astype(BF16)
    twice = mm(pick, hidden, 1, 1).astype(BF16)
    half = out_ref.shape[1]
    even = lax.broadcasted_iota(jnp.int32, (128, half), 0) % 2 == 0
    first = mm(twice, w_ref[:, 0:half])
    second = mm(twice, w_ref[:, half:2 * half])
    out_ref[...] = jnp.where(even, first, second).astype(BF16)


def total_kernel(parts_ref, out_ref, wide_ref):
    acc = parts_ref[0].astype(F32)
    for i in range(1, parts_ref.shape[0]):
        acc = acc + parts_ref[i].astype(F32)
    half = acc.shape[1]
    for j in range(half // 128):
        wide_ref[j] = acc[:, j * 128:(j + 1) * 128]
        for part in range(2):
            out_ref[:, part * half + j * 128:part * half + (j + 1) * 128] = (
                wide_ref[j, pl.ds(part, 4, stride=2), :].astype(BF16))


def shards(tokens, w_qkv, lr_weight, lr_base, conv_weight, w_init, w_out):
    width = tokens.shape[1]
    half = width // 2
    inner = w_qkv.shape[1]
    n_seq = lax.axis_size("seq")
    n_head = lax.axis_size("head")
    params = pltpu.CompilerParams(vmem_limit_bytes=24 * 1024 * 1024)
    vmem = pl.BlockSpec(memory_space=pltpu.VMEM)
    hbm = pl.BlockSpec(memory_space=pl.ANY)

    folded = pl.pallas_call(
        fold_kernel,
        out_shape=jax.ShapeDtypeStruct((n_head, 8, half), BF16),
        in_specs=[vmem],
        out_specs=hbm,
        scratch_shapes=[
            pltpu.VMEM((half // 128, 8, 128), F32),
            pltpu.VMEM((8, half), BF16),
            pltpu.SemaphoreType.DMA((n_head,)),
        ],
        compiler_params=params,
        name="fold",
    )(tokens)
    own = lax.all_to_all(folded, "head", 0, 0)
    weights, lr_rows, taps, base = pl.pallas_call(
        prepare_kernel,
        out_shape=(
            jax.ShapeDtypeStruct((3, 128, width), BF16),
            jax.ShapeDtypeStruct((16, width), BF16),
            jax.ShapeDtypeStruct((256, 2 * KERNEL), F32),
            jax.ShapeDtypeStruct((8, 128), F32),
        ),
        in_specs=[hbm] + [vmem] * 3,
        out_specs=(vmem,) * 4,
        scratch_shapes=[pltpu.SemaphoreType.DMA(())],
        compiler_params=params,
        name="prepare",
    )(w_qkv, lr_weight, conv_weight, lr_base.reshape(1, lr_base.shape[0]))
    own, weights = lax.optimization_barrier((own, weights))
    swap = [(i, i ^ 1) for i in range(n_seq)]
    mate = lax.ppermute(own, "seq", swap)
    tail = own[n_head - 1]
    halo0 = lax.ppermute(tail, "seq", [(i, i + 1) for i in range(1, n_seq - 1, 2)])
    halo1 = lax.ppermute(tail, "seq", [(i, i + 2) for i in range(1, n_seq - 2, 2)])
    tails = pl.pallas_call(
        tail_kernel,
        out_shape=jax.ShapeDtypeStruct((16, width), BF16),
        in_specs=[vmem] * 2,
        out_specs=vmem,
        scratch_shapes=[pltpu.VMEM((half // 128, 32, 128), F32)],
        compiler_params=params,
        cost_estimate=pl.CostEstimate(flops=20_000_000_000, transcendentals=0, bytes_accessed=0),
        name="tails",
    )(halo0, halo1)
    send, qeff, oeff = pl.pallas_call(
        local_kernel,
        out_shape=(
            jax.ShapeDtypeStruct((160, 128), BF16),
            jax.ShapeDtypeStruct((2, 128, 128), BF16),
            jax.ShapeDtypeStruct((2, 96, 128), F32),
        ),
        in_specs=[vmem] * 7,
        out_specs=(vmem, vmem, vmem),
        scratch_shapes=[
            pltpu.VMEM((half // 128, 128, 128), F32),
            pltpu.VMEM((256, width), BF16),
        ],
        compiler_params=params,
        name="local",
    )(own.reshape(n_head * 8, half), mate.reshape(n_head * 8, half), tails, weights, lr_rows, taps, base)

    groups = [[2 * j + (c + j) % 2 for j in range(n_seq // 2)] for c in range(2)]
    received = lax.all_gather(send, "seq", axis_index_groups=groups)
    rows = pl.pallas_call(
        chain_kernel,
        out_shape=jax.ShapeDtypeStruct((128, 128), F32),
        in_specs=[vmem] * 4,
        out_specs=vmem,
        compiler_params=params,
        name="chain",
    )(received, qeff, oeff, w_init)
    other = lax.ppermute(rows, "seq", swap)
    partial = pl.pallas_call(
        output_kernel,
        out_shape=jax.ShapeDtypeStruct((n_head * 8, half), BF16),
        in_specs=[vmem] * 3,
        out_specs=vmem,
        compiler_params=params,
        name="output",
    )(rows, other, w_out)
    parts = lax.all_to_all(partial.reshape(n_head, 8, half), "head", 0, 0)
    return pl.pallas_call(
        total_kernel,
        out_shape=jax.ShapeDtypeStruct(tokens.shape, BF16),
        in_specs=[vmem],
        out_specs=vmem,
        scratch_shapes=[pltpu.VMEM((half // 128, 8, 128), F32)],
        compiler_params=params,
        name="total",
    )(parts)


def solution(mesh):
    placed = (
        P(("seq", "head"), None),
        P(None, "head", None),
        P("head", None),
        P("head"),
        P(None, None, "head"),
        P(None, "head", None, None),
        P("head", None),
    )
    return jax.shard_map(
        shards, mesh=mesh, in_specs=placed, out_specs=P(("seq", "head"), None), check_vma=False
    )
```
